32 devices in a mesh: alpha: 16 (over z, y, x), beta: 2 (over core).
Axes of the slice: x: 2, y: 2, z: 4, core: 2. Of those that a mesh axis runs over, the one named last changes fastest.
Arguments:
- coeffs: bfloat16 [1, 2048, 4096], P(None, 'alpha', 'beta'), may hold values from -6 to 6
- beta_list: int32 [32, 8], P('beta'), may hold values from 0 to 31
- beta_kind: int32 [32, 8], P('beta'), may hold values from 0 to 7
- opp_beta_kind: int32 [32, 8], P('beta'), may hold values from 0 to 7
- alpha_list: int32 [16, 4], replicated, may hold values from 0 to 15, as said below
- alpha_kind: int32 [16, 4], replicated, may hold values from 0 to 7
- opp_list: int32 [16, 3], replicated, may hold values from 0 to 15, as said below
- opp_kind: int32 [16, 3], replicated, may hold values from 0 to 7
- beta_table: bfloat16 [8, 128, 128], replicated, may hold values from -0.1875 to 0.1875
- alpha_table: bfloat16 [8, 128, 128], replicated, may hold values from -0.25 to 0.25
- opp_alpha_table: bfloat16 [8, 128, 128], replicated, may hold values from -0.3125 to 0.3125
- opp_beta_table: bfloat16 [8, 128, 128], replicated, may hold values from -0.1875 to 0.1875
Outputs:
- sigma_out: bfloat16 [1, 2048, 4096], P(None, 'alpha', 'beta')
The draws below stay inside these ranges and needn't reach their ends.
Inputs may be any that keep to these rules, and one draw needn't show every extreme that they name: `alpha_list`: each entry of row i lies within 3 of i; the entries of a row are distinct. `opp_list`: each entry of row i lies within 3 of i; the entries of a row are distinct.
All inputs are finite; a program needn't handle non-finite values.
Results may differ from the reference program's by a relative error of at most 0.0034.
Values may be sent and summed in bfloat16 or wider, within the bound.
A program may use at most 128 MiB of HBM per device.

```python
import jax
import jax.numpy as jnp
from jax import lax

TILE = 128
NB = 4096
ROOTS = 1
BETA_LINKS = 8
ALPHA_LINKS = 4
OPP_LINKS = 3
KINDS = 8
REACH = 3
NA = 2048


def pick_nearby(key, count):
    block_count = NA // TILE
    span_count = 2 * REACH + 1
    offsets = jnp.arange(span_count, dtype=jnp.int32) - REACH
    row_ids = jnp.arange(block_count, dtype=jnp.int32)[:, None]
    target = row_ids + offsets[None, :]
    inside = (target >= 0) & (target < block_count)
    scores = jax.random.randint(key, (block_count, span_count), 0, 1 << 20, dtype=jnp.int32) * span_count + jnp.arange(span_count, dtype=jnp.int32)[None, :]
    scores = jnp.where(inside, scores + 1, 0)
    unused, chosen = lax.top_k(scores, count)
    return jnp.take_along_axis(target, chosen, axis=1).astype(jnp.int32)


def draw_alpha_list(key, part):
    return pick_nearby(jax.random.fold_in(key, 11), ALPHA_LINKS)


def draw_opp_list(key, part):
    return pick_nearby(jax.random.fold_in(key, 23), OPP_LINKS)


def set_ends(array, own_key, smallest, high):
    longest = array.shape.index(max(array.shape))
    spots = []
    for shift in (0, 1):
        where = [jax.random.randint(jax.random.fold_in(own_key, axis), (), 0, length) for axis, length in enumerate(array.shape)]
        where[longest] = (where[longest] + shift) % array.shape[longest]
        spots.append(tuple(where))
    return array.at[spots[0]].set(smallest).at[spots[1]].set(high)


def block_scale(own_key, shape, pieces, least, top_value):
    def one(dim, parts):
        heights = jax.random.uniform(jax.random.fold_in(jax.random.fold_in(own_key, 6), dim), (parts,), jnp.float32, least / len(pieces), top_value / len(pieces))
        return jnp.repeat(jnp.exp(heights), shape[dim] // parts).reshape((-1,) + (1,) * (len(shape) - dim - 1))

    level = one(*pieces[0])
    for cut in pieces[1:]:
        level = level * one(*cut)
    return level


def normal_values(own_key, extent, spread, limit, split=(), kind=jnp.bfloat16):
    drawn = jax.random.normal(own_key, extent, jnp.float32) * spread
    if len(split) > 0:
        drawn = block_scale(own_key, extent, split, -0.22, 0.18) * drawn
    return jnp.clip(drawn, min=-limit, max=limit).astype(kind)


def setup_inputs(seed: int = 0) -> dict:
    keys = jax.random.split(jax.random.key(seed), 13)
    return {
        "coeffs": normal_values(keys[0], (ROOTS, NA, NB), 1.0, 6.0, ((1, 16), (2, 2))),
        "beta_list": set_ends(jax.random.randint(keys[1], (NB // TILE, BETA_LINKS), 0, NB // TILE), jax.random.fold_in(keys[1], 1), 0, (NB // TILE) - 1).astype(jnp.int32),
        "beta_kind": set_ends(jax.random.randint(keys[2], (NB // TILE, BETA_LINKS), 0, KINDS), jax.random.fold_in(keys[2], 1), 0, KINDS - 1).astype(jnp.int32),
        "opp_beta_kind": set_ends(jax.random.randint(keys[3], (NB // TILE, BETA_LINKS), 0, KINDS), jax.random.fold_in(keys[3], 1), 0, KINDS - 1).astype(jnp.int32),
        "alpha_list": draw_alpha_list(jax.random.fold_in(keys[12], 71), 0),
        "alpha_kind": set_ends(jax.random.randint(keys[5], (NA // TILE, ALPHA_LINKS), 0, KINDS), jax.random.fold_in(keys[5], 1), 0, KINDS - 1).astype(jnp.int32),
        "opp_list": draw_opp_list(jax.random.fold_in(keys[12], 71), 0),
        "opp_kind": set_ends(jax.random.randint(keys[7], (NA // TILE, OPP_LINKS), 0, KINDS), jax.random.fold_in(keys[7], 1), 0, KINDS - 1).astype(jnp.int32),
        "beta_table": normal_values(keys[8], (KINDS, TILE, TILE), (TILE * BETA_LINKS) ** -0.5, 0.1875),
        "alpha_table": normal_values(keys[9], (KINDS, TILE, TILE), (TILE * ALPHA_LINKS) ** -0.5, 0.25),
        "opp_alpha_table": normal_values(keys[10], (KINDS, TILE, TILE), (TILE * OPP_LINKS) ** -0.5, 0.3125),
        "opp_beta_table": normal_values(keys[11], (KINDS, TILE, TILE), (TILE * BETA_LINKS) ** -0.5, 0.1875),
    }


def beta_apply(row_data, sources, kind_ids, tile_table):
    root_count, row_count, col_count = row_data.shape
    tile_size = tile_table.shape[1]
    tiled = row_data.reshape(root_count, row_count, col_count // tile_size, tile_size)
    summed = jnp.zeros((root_count, row_count, sources.shape[0], tile_size), jnp.float32)
    for link in range(sources.shape[1]):
        picked = jnp.take(tiled, sources[:, link], axis=2).astype(jnp.float32)
        tile_sets = jnp.take(tile_table, kind_ids[:, link], axis=0).astype(jnp.float32)
        summed = summed + jnp.einsum("rajt,jst->rajs", picked, tile_sets, precision=lax.Precision.HIGHEST)
    return summed.reshape(root_count, row_count, -1)


def alpha_sum(blocks, sources, kind_ids, tile_table):
    summed = jnp.zeros((blocks.shape[0], blocks.shape[2], blocks.shape[3]), jnp.float32)
    for link in range(sources.shape[0]):
        picked = lax.dynamic_index_in_dim(blocks, sources[link], 1, keepdims=False).astype(jnp.float32)
        tile_one = lax.dynamic_index_in_dim(tile_table, kind_ids[link], 0, keepdims=False).astype(jnp.float32)
        summed = summed + jnp.einsum("st,rtc->rsc", tile_one, picked, precision=lax.Precision.HIGHEST)
    return summed


def reference(coeffs, beta_list, beta_kind, opp_beta_kind, alpha_list, alpha_kind, opp_list, opp_kind, beta_table, alpha_table, opp_alpha_table, opp_beta_table):
    root_count, alpha_count, beta_count = coeffs.shape
    tile_size = alpha_table.shape[1]
    block_count = alpha_count // tile_size
    blocks = coeffs.reshape(root_count, block_count, tile_size, beta_count)

    def one_block(block):
        own_rows = lax.dynamic_index_in_dim(blocks, block, 1, keepdims=False)
        beta_part = beta_apply(own_rows, beta_list, beta_kind, beta_table)
        alpha_part = alpha_sum(blocks, alpha_list[block], alpha_kind[block], alpha_table)
        half_sum = alpha_sum(blocks, opp_list[block], opp_kind[block], opp_alpha_table).astype(jnp.bfloat16)
        mixed_part = beta_apply(half_sum, beta_list, opp_beta_kind, opp_beta_table)
        return (beta_part + alpha_part + mixed_part).astype(jnp.bfloat16)

    result = lax.map(one_block, jnp.arange(block_count, dtype=jnp.int32))
    return jnp.transpose(result, (1, 0, 2, 3)).reshape(root_count, alpha_count, beta_count)
```

```python
import functools

import jax
import jax.numpy as jnp
from jax import lax
from jax.experimental import pallas as pl
from jax.experimental.pallas import tpu as pltpu
from jax.sharding import PartitionSpec as P

GROUP = 4
AHEAD = 6
FORWARD, STRIDE = 12, 10
DELAY = 3
SHIFT = 1.5
BF16, F32 = jnp.bfloat16, jnp.float32
LOW, HIGH, DIAG = range(3)


def picked_tile(block, lists, kinds, table, source):
    kind, found = jnp.int32(0), jnp.int32(0)
    for link in range(lists.shape[0]):
        hit = (lists[link, block] == source).astype(jnp.int32)
        kind += hit * kinds[link, block]
        found += hit
    return table[kind].astype(F32) * found.astype(F32)


def order_of(summed, relayed):
    spread = [(2 * g + 1, summed, "s", g) for g in range(summed // 2)]
    spread += [(2 * g + SHIFT, relayed, "r", g) for g in range(relayed // 2)]
    return [(kind, g) for _, _, kind, g in sorted(spread, key=lambda one: one[0] / one[1])]


def make_plans(summed, relayed):
    wanted = {LOW: [], HIGH: []}
    for kind, g in order_of(summed, relayed):
        first = 2 * g + (summed if kind == "r" else 0)
        wanted[LOW] += [first, first + 1]
        wanted[HIGH] += [first + 1, first]
    late = [c for c in wanted[HIGH] if c >= summed and c % 2 == 0]
    own = {LOW: list(wanted[LOW]), HIGH: [c for c in wanted[HIGH] if c not in late] + late}
    relays = {LOW: [c for c in wanted[HIGH] if c % 2 == 1], HIGH: [c for c in wanted[LOW] if c % 2 == 0]}
    plans, own_at, forward_at = ([], []), ({}, {}), []
    passed = hopped = n = 0
    while own[LOW] or own[HIGH] or relays[LOW] or relays[HIGH] or hopped < relayed:
        for link in (LOW, HIGH):
            other = HIGH if link == LOW else LOW
            due = passed < relayed and n >= FORWARD + STRIDE * passed // 4
            ready = relays[link] and own_at[other].get(relays[link][0], n) + AHEAD <= n
            spare = not own[link] or own[link][0] in late
            if ready:
                plans[link].append(("r", relays[link].pop(0)))
            elif link == HIGH and passed < relayed and (due or spare):
                plans[link].append(("f", summed + passed))
                forward_at.append(n)
                passed += 1
            elif own[link]:
                own_at[link][own[link][0]] = n
                plans[link].append(("o", own[link].pop(0)))
            elif link == LOW and hopped < passed and forward_at[hopped] + AHEAD <= n:
                plans[link].append(("h", summed + hopped))
                hopped += 1
            else:
                plans[link].append((None, None))
        n += 1
    return plans


def slots_of(plans):
    slots, most = ([], []), 0
    for link, plan in enumerate(plans):
        held = []
        for n, (kind, _) in enumerate(plan):
            sure = [k for k in range(n - AHEAD + 1) if plan[k][0] in ("o", "r")]
            free = sure[-1] - AHEAD if sure else -1
            if kind in ("o", "r", "f"):
                spot = next((k for k, user in enumerate(held) if user <= free), len(held))
                held[spot : spot + 1] = [n]
                slots[link].append(spot)
            else:
                slots[link].append(None)
        most = max(most, len(held))
    return slots, most


def closing(plans, summed, relayed):
    at = [{item: n for n, item in enumerate(plan)} for plan in plans]
    last = len(plans[LOW]) - 1
    free, ends = 0, []
    events = [(n, c) for (kind, c), n in at[LOW].items() if kind == "o" and c >= summed]
    for g in range(summed // 2):
        events.append((max(at[LOW]["r", 2 * g + 1], at[HIGH]["r", 2 * g]), 2 * g))
    for n, c in sorted(events):
        free = max(free, n) + (1 if c >= summed else 4)
        if c < summed:
            ends.append((free + DELAY, c // 2))
    for g in range(summed // 2, (summed + relayed) // 2):
        ends.append((max(n for link in (LOW, HIGH) for (_, c), n in at[link].items() if c in (2 * g, 2 * g + 1)), g))
    return [(min(n, last), g) for n, g in sorted(ends)]


def kernel(
    group_count,
    beta_list_hbm,
    beta_kind_hbm,
    opp_beta_kind_hbm,
    alpha_list_hbm,
    alpha_kind_hbm,
    opp_list_hbm,
    opp_kind_hbm,
    coeffs_hbm,
    beta_table_hbm,
    alpha_table_hbm,
    opp_alpha_table_hbm,
    opp_beta_table_hbm,
    out,
    beta_list,
    beta_kind,
    opp_beta_kind,
    alpha_list,
    alpha_kind,
    opp_list,
    opp_kind,
    coeffs,
    tables,
    plane,
    cross,
    sums,
    staged,
    passing,
    whole,
    half,
    acc,
    mine,
    tiles,
    onward,
    load_sem,
    own_send,
    plane_recv,
    relay_send,
    z_send,
    cross_recv,
    sum_send,
    pass_send,
    pass_recv,
    forward_send,
    hop_send,
    pair_send,
    pair_recv,
    half_send,
    half_recv,
):
    rows, cols = coeffs.shape
    kinds, tile = tables.shape[1:3]
    count = cols // tile
    relayed = count // 2
    summed = count - relayed
    plans = make_plans(summed, relayed)
    slots, _ = slots_of(plans)
    beta_table, alpha_table, opp_alpha_table, opp_beta_table = (tables.at[k] for k in range(4))
    me, core = lax.axis_index("alpha"), lax.axis_index("beta")
    z, p = me // GROUP, me % GROUP
    x, y = p % 2, p // 2
    places = (p + 1 - 2 * x, p + 2 - 4 * y, 3 - p)
    mates = tuple(z * GROUP + q for q in places)
    steps = (1 - 2 * x, 1 - 2 * y, 1 - 2 * y)
    middle = x + y == 1
    corner = jnp.logical_not(middle)

    def inside(group):
        return (group >= 0) & (group < group_count)

    has_out = [inside(z + step) for step in steps]
    has_in = [inside(z - step) for step in steps]

    def chip(index):
        return (index, core)

    pair = (me, 1 - core)

    def send(src, dst, send_sem, recv_sem, device):
        return pltpu.make_async_remote_copy(
            src_ref=src,
            dst_ref=dst,
            send_sem=send_sem,
            recv_sem=recv_sem,
            device_id=device,
            device_id_type=pl.DeviceIdType.MESH,
        )

    def sent(ref, sem):
        send(ref, ref, sem, sem, pair).wait_send()

    def arrived(ref, sem):
        send(ref, ref, sem, sem, pair).wait_recv()

    def columns(c):
        return pl.ds(c * tile, tile)

    def wide(g):
        return pl.ds(g * 2 * tile, 2 * tile)

    def both(g):
        return pl.ds(2 * g, 2)

    def own_copy(to, n, c):
        return send(
            coeffs.at[:, columns(c)],
            plane.at[to, c],
            own_send.at[to],
            plane_recv.at[to, slots[to][n]],
            chip(mates[to]),
        )

    def relay_copy(to, n, c):
        return send(
            plane.at[HIGH if to == LOW else LOW, c],
            plane.at[DIAG, c],
            relay_send,
            plane_recv.at[to, slots[to][n]],
            chip(mates[to]),
        )

    def z_copy(r, c):
        return send(
            plane.at[r, c],
            cross.at[r, c],
            z_send.at[r],
            cross_recv.at[min(r, 1), c // 2],
            chip(me + GROUP * steps[r]),
        )

    def sum_copy(c):
        return send(staged.at[c], sums.at[c], sum_send, cross_recv.at[0, c // 2], chip(me + GROUP * steps[LOW]))

    def pass_copy(c):
        k = c - summed
        return send(
            coeffs.at[:, columns(c)], passing.at[k], pass_send, pass_recv.at[k // 2], chip(me - GROUP * steps[HIGH])
        )

    def forward_copy(n, c):
        return send(
            passing.at[c - summed],
            cross.at[HIGH, c],
            forward_send,
            plane_recv.at[HIGH, slots[HIGH][n]],
            chip(mates[HIGH]),
        )

    def hop_copy(c):
        return send(cross.at[HIGH, c], cross.at[DIAG, c], hop_send, cross_recv.at[1, c // 2], chip(mates[LOW]))

    def half_copy(g):
        part = half.at[pl.ds(core * count + 2 * g, 2)]
        return send(part, part, half_send, half_recv, pair)

    def pair_copy(t):
        part = coeffs_hbm.at[:, pl.ds(t * tile, tile)]
        return send(part, whole.at[core * count + t], pair_send, pair_recv, pair)

    lists = (
        (alpha_list_hbm, alpha_list),
        (alpha_kind_hbm, alpha_kind),
        (opp_list_hbm, opp_list),
        (opp_kind_hbm, opp_kind),
        (beta_list_hbm, beta_list),
        (beta_kind_hbm, beta_kind),
        (opp_beta_kind_hbm, opp_beta_kind),
    )
    load_coeffs = pltpu.make_async_copy(coeffs_hbm, coeffs, load_sem.at[0])
    load_lists = [pltpu.make_async_copy(src, dst, load_sem.at[2 + k]) for k, (src, dst) in enumerate(lists)]
    load_coeffs.start()
    for load in load_lists:
        load.start()
    for k, src in enumerate((beta_table_hbm, alpha_table_hbm, opp_alpha_table_hbm, opp_beta_table_hbm)):
        pltpu.make_async_copy(src, tables.at[k], load_sem.at[1]).start()

    barrier = pltpu.get_barrier_semaphore()
    for device in (chip(mates[LOW]), chip(mates[HIGH]), pair):
        pl.semaphore_signal(barrier, inc=1, device_id=device, device_id_type=pl.DeviceIdType.MESH)
    up, down = inside(z + 1), inside(z - 1)
    for there, offset in ((up, GROUP), (down, -GROUP)):

        @pl.when(there)
        def _():
            pl.semaphore_signal(
                barrier, inc=1, device_id=chip(me + offset), device_id_type=pl.DeviceIdType.MESH
            )

    for load in load_lists:
        load.wait()
    load_coeffs.wait()
    pltpu.make_async_copy(tables, tables, load_sem.at[1]).wait()

    pl.semaphore_wait(barrier, 3 + up.astype(jnp.int32) + down.astype(jnp.int32))

    for n in range(AHEAD):
        for link in (LOW, HIGH):
            own_copy(link, n, plans[link][n][1]).start()

    @pl.when(has_in[HIGH])
    def _():
        for c in range(summed, count):
            pass_copy(c).start()

    for t in range(count):
        pair_copy(t).start()
    for t in range(count):
        whole[core * count + t] = coeffs[:, t * tile : (t + 1) * tile]

    for r in range(3):

        @pl.when(jnp.logical_not(has_in[r]))
        def _():
            cross[r] = jnp.zeros_like(cross[r])

    @pl.when(corner & jnp.logical_not(has_in[LOW]))
    def _():
        sums[...] = jnp.zeros_like(sums)

    sources = [me, *mates] + [mates[r] - GROUP * steps[r] for r in range(3)]
    for slot, source in enumerate(sources):
        at = pl.ds(slot * tile, tile)
        tiles[:tile, at] = picked_tile(me, alpha_list, alpha_kind, alpha_table, source).astype(BF16)
        tiles[tile:, at] = picked_tile(me, opp_list, opp_kind, opp_alpha_table, source).astype(BF16)

    summing = corner & has_out[LOW]

    @pl.when(summing)
    def _():
        target = me + GROUP * steps[LOW]
        for slot, source in enumerate(mates):
            at = pl.ds(slot * tile, tile)
            onward[:tile, at] = picked_tile(target, alpha_list, alpha_kind, alpha_table, source).astype(BF16)
            onward[tile:, at] = picked_tile(target, opp_list, opp_kind, opp_alpha_table, source).astype(BF16)

    def product(weights, first, blocks):
        return jnp.dot(
            weights[:, first * tile : (first + len(blocks)) * tile],
            jnp.concatenate(blocks, axis=0),
            preferred_element_type=F32,
        )

    def wide_block(ref, r, g):
        return jnp.concatenate([ref[r, 2 * g], ref[r, 2 * g + 1]], axis=1)

    def beta_apply(data, kind, table, j):
        left, right = [], []
        for link in range(beta_list.shape[0]):
            left.append(data[beta_list[link, j]])
            right.append(table[kind[link, j]])
        return lax.dot_general(
            jnp.concatenate(left, axis=1),
            jnp.concatenate(right, axis=1),
            (((1,), (1,)), ((), ())),
            preferred_element_type=F32,
        )

    def same_spin(j):
        mine[:, columns(j)] = beta_apply(whole, beta_kind, beta_table, j)

    def in_plane(g):
        acc[:, wide(g)] = product(
            tiles, 0, [coeffs[:, wide(g)], *(wide_block(plane, r, g) for r in range(3))]
        )

    def cross_wait(first, g, there=True):
        @pl.when(has_in[first] & there)
        def _():
            if first == LOW or 2 * g >= summed:
                arrived(cross.at[LOW if first == LOW else DIAG, both(g)], cross_recv.at[first, g])
            else:
                arrived(cross.at[pl.ds(HIGH, 2), both(g)], cross_recv.at[first, g])

    def settle(g, added):
        total = added
        for t in range(2):
            half[core * count + 2 * g + t] = total[tile:, t * tile : (t + 1) * tile].astype(BF16)
        mine[:, wide(g)] += total[:tile]

    def close(g):
        there = True if 2 * g >= summed else middle
        cross_wait(LOW, g, there)
        cross_wait(HIGH, g, there)
        if 2 * g < summed:

            @pl.when(corner & has_in[LOW])
            def _():
                arrived(sums.at[both(g)], cross_recv.at[0, g])

        if 2 * g >= summed:
            settle(
                g,
                product(
                    tiles,
                    0,
                    [
                        coeffs[:, wide(g)],
                        *(wide_block(plane, r, g) for r in range(3)),
                        *(wide_block(cross, r, g) for r in range(3)),
                    ],
                ),
            )
        else:

            @pl.when(middle)
            def _():
                settle(g, acc[:, wide(g)] + product(tiles, 4, [wide_block(cross, r, g) for r in range(3)]))

            @pl.when(corner)
            def _():
                settle(g, acc[:, wide(g)] + jnp.concatenate([sums[2 * g], sums[2 * g + 1]], axis=1).astype(F32))

        half_copy(g).start()

    def sum_up(g):
        @pl.when(summing)
        def _():
            found = product(onward, 0, [wide_block(plane, r, g) for r in range(3)]).astype(BF16)
            for t in range(2):
                staged[2 * g + t] = found[:, t * tile : (t + 1) * tile]
                sum_copy(2 * g + t).start()

    seen = set()

    def take(link, n):
        kind, c = plans[link][n]
        if kind == "o":
            own_copy(link, n, c).wait_recv()
            if link == LOW:
                there = has_out[LOW] if c >= summed else has_out[LOW] & middle
            else:
                there = has_out[HIGH] & middle
            if link == LOW or c < summed:

                @pl.when(there)
                def _():
                    z_copy(link, c).start()

        elif kind == "r":
            relay_copy(link, n, c).wait_recv()

            @pl.when(middle & has_out[DIAG])
            def _():
                z_copy(DIAG, c).start()

            seen.add(c)
            if c < summed and c ^ 1 in seen:
                sum_up(c // 2)
                in_plane(c // 2)
        elif kind == "f":

            @pl.when(has_in[HIGH])
            def _():
                forward_copy(n, c).wait_recv()

    def issue(link, n):
        kind, c = plans[link][n]
        if kind == "o":
            own_copy(link, n, c).start()
        elif kind == "r":
            relay_copy(link, n, c).start()
        elif kind == "f":

            @pl.when(has_out[HIGH])
            def _():
                if c % 2 == 0:
                    k = c - summed
                    arrived(passing.at[pl.ds(k, 2)], pass_recv.at[k // 2])
                forward_copy(n, c).start()

        elif kind == "h":

            @pl.when(middle & has_in[HIGH])
            def _():
                hop_copy(c).start()

    last = len(plans[LOW])
    after = {i: [] for i in range(-1, last)}

    def put(i, what, *args):
        after[i].append((what, args))

    for j in range(count):
        put(-1, same_spin, j)
    for n, g in closing(plans, summed, relayed):
        put(n, close, g)

    arrived(whole.at[pl.ds((1 - core) * count, count)], pair_recv)
    for i in range(-1, last):
        if i >= 0:
            for link in (LOW, HIGH):
                take(link, i)
            if i + AHEAD < last:
                for link in (LOW, HIGH):
                    issue(link, i + AHEAD)
        for what, args in after[i]:
            what(*args)

    arrived(half.at[pl.ds((1 - core) * count, count)], half_recv)
    for j in range(count):
        mixed = beta_apply(half, opp_beta_kind, opp_beta_table, j)
        out[:, columns(j)] = (mine[:, columns(j)] + mixed).astype(BF16)

    sent(coeffs, own_send.at[LOW])
    sent(coeffs, own_send.at[HIGH])
    sent(whole.at[pl.ds(0, count)], pair_send)
    sent(half.at[pl.ds(0, count)], half_send)
    sent(plane.at[DIAG], relay_send)

    @pl.when(has_in[HIGH])
    def _():
        sent(passing, pass_send)

    @pl.when(has_out[HIGH])
    def _():
        sent(passing, forward_send)

    @pl.when(middle & has_in[HIGH])
    def _():
        sent(passing, hop_send)

    @pl.when(middle & has_out[LOW])
    def _():
        sent(plane.at[LOW], z_send.at[LOW])

    @pl.when(middle & has_out[HIGH])
    def _():
        sent(plane.at[HIGH, pl.ds(0, summed)], z_send.at[HIGH])
        sent(plane.at[DIAG], z_send.at[DIAG])

    @pl.when(summing)
    def _():
        sent(plane.at[LOW, pl.ds(0, relayed)], z_send.at[LOW])
        sent(staged, sum_send)


def local(group_count, coeffs, *rest):
    lists, tables = rest[:7], rest[7:]
    flat = coeffs.reshape(coeffs.shape[1:])
    rows, cols = flat.shape
    kinds, tile = tables[0].shape[:2]
    count = cols // tile
    relayed, groups = count // 2, count // 2
    summed = count - relayed
    operands = tuple(
        pltpu.with_memory_space_constraint(one, pltpu.HBM) for one in (*(one.T for one in lists), flat, *tables)
    )
    in_lists = [pltpu.SMEM(one.shape, one.dtype) for one in operands[:7]]
    dma = pltpu.SemaphoreType.DMA
    result = pl.pallas_call(
        functools.partial(kernel, group_count),
        out_shape=jax.ShapeDtypeStruct((rows, cols), BF16),
        in_specs=[pl.BlockSpec(memory_space=pltpu.HBM)] * len(operands),
        out_specs=pl.BlockSpec(memory_space=pltpu.VMEM),
        scratch_shapes=[
            *in_lists,
            pltpu.VMEM((rows, cols), BF16),
            pltpu.VMEM((len(tables), *tables[0].shape), BF16),
            pltpu.VMEM((3, count, rows, tile), BF16),
            pltpu.VMEM((3, count, rows, tile), BF16),
            pltpu.VMEM((summed, 2 * rows, tile), BF16),
            pltpu.VMEM((summed, 2 * rows, tile), BF16),
            pltpu.VMEM((relayed, rows, tile), BF16),
            pltpu.VMEM((2 * count, rows, tile), BF16),
            pltpu.VMEM((2 * count, rows, tile), BF16),
            pltpu.VMEM((2 * tile, cols), F32),
            pltpu.VMEM((rows, cols), F32),
            pltpu.VMEM((2 * tile, 7 * tile), BF16),
            pltpu.VMEM((2 * tile, 3 * tile), BF16),
            dma((9,)),
            dma((2,)),
            dma((2, slots_of(make_plans(summed, relayed))[1])),
            dma,
            dma((3,)),
            dma((2, groups)),
            dma,
            dma,
            dma((relayed // 2,)),
            dma,
            dma,
            dma,
            dma,
            dma,
            dma,
        ],
        compiler_params=pltpu.CompilerParams(
            collective_id=0, has_side_effects=True, vmem_limit_bytes=20000 * 1024
        ),
    )(*operands)
    return result.reshape(coeffs.shape)


def solution(mesh):
    halves = P("beta", None)
    return jax.shard_map(
        functools.partial(local, mesh.shape["alpha"] // GROUP),
        mesh=mesh,
        in_specs=(P(None, "alpha", "beta"), halves, halves, halves) + (P(),) * 8,
        out_specs=P(None, "alpha", "beta"),
        check_vma=False,
    )
```

```python
import functools

import jax
import jax.numpy as jnp
from jax import lax
from jax.experimental import pallas as pl
from jax.experimental.pallas import tpu as pltpu
from jax.sharding import PartitionSpec as P

GROUP = 4
AHEAD = 6
FORWARD, STRIDE = 15, 7
DELAY = 3
SHIFT = 3
BF16, F32 = jnp.bfloat16, jnp.float32
LOW, HIGH, DIAG = range(3)


def picked_tile(block, lists, kinds, table, source):
    kind, found = jnp.int32(0), jnp.int32(0)
    for link in range(lists.shape[0]):
        hit = (lists[link, block] == source).astype(jnp.int32)
        kind += hit * kinds[link, block]
        found += hit
    return table[kind].astype(F32) * found.astype(F32)


def order_of(summed, relayed):
    spread = [(2 * g + 1, summed, "s", g) for g in range(summed // 2)]
    spread += [(2 * g + SHIFT, relayed, "r", g) for g in range(relayed // 2)]
    return [(kind, g) for _, _, kind, g in sorted(spread, key=lambda one: one[0] / one[1])]


def make_plans(summed, relayed):
    wanted = {LOW: [], HIGH: []}
    for kind, g in order_of(summed, relayed):
        first = 2 * g + (summed if kind == "r" else 0)
        wanted[LOW] += [first, first + 1]
        wanted[HIGH] += [first + 1, first]
    late = [c for c in wanted[HIGH] if c >= summed and c % 2 == 0]
    own = {LOW: list(wanted[LOW]), HIGH: [c for c in wanted[HIGH] if c not in late] + late}
    relays = {LOW: [c for c in wanted[HIGH] if c % 2 == 1], HIGH: [c for c in wanted[LOW] if c % 2 == 0]}
    plans, own_at, forward_at = ([], []), ({}, {}), []
    passed = hopped = n = 0
    while own[LOW] or own[HIGH] or relays[LOW] or relays[HIGH] or hopped < relayed:
        for link in (LOW, HIGH):
            other = HIGH if link == LOW else LOW
            due = passed < relayed and n >= FORWARD + STRIDE * passed // 4
            ready = relays[link] and own_at[other].get(relays[link][0], n) + AHEAD <= n
            spare = not own[link] or own[link][0] in late
            if ready:
                plans[link].append(("r", relays[link].pop(0)))
            elif link == HIGH and passed < relayed and (due or spare):
                plans[link].append(("f", summed + passed))
                forward_at.append(n)
                passed += 1
            elif own[link]:
                own_at[link][own[link][0]] = n
                plans[link].append(("o", own[link].pop(0)))
            elif link == LOW and hopped < passed and forward_at[hopped] + AHEAD <= n:
                plans[link].append(("h", summed + hopped))
                hopped += 1
            else:
                plans[link].append((None, None))
        n += 1
    return plans


def slots_of(plans):
    slots, most = ([], []), 0
    for link, plan in enumerate(plans):
        held = []
        for n, (kind, _) in enumerate(plan):
            sure = [k for k in range(n - AHEAD + 1) if plan[k][0] in ("o", "r")]
            free = sure[-1] - AHEAD if sure else -1
            if kind in ("o", "r", "f"):
                spot = next((k for k, user in enumerate(held) if user <= free), len(held))
                held[spot : spot + 1] = [n]
                slots[link].append(spot)
            else:
                slots[link].append(None)
        most = max(most, len(held))
    return slots, most


def closing(plans, summed, relayed):
    at = [{item: n for n, item in enumerate(plan)} for plan in plans]
    last = len(plans[LOW]) - 1
    free, ends = 0, []
    events = [(n, c) for (kind, c), n in at[LOW].items() if kind == "o" and c >= summed]
    for g in range(summed // 2):
        events.append((max(at[LOW]["r", 2 * g + 1], at[HIGH]["r", 2 * g]), 2 * g))
    for n, c in sorted(events):
        free = max(free, n) + (1 if c >= summed else 4)
        if c < summed:
            ends.append((free + DELAY, c // 2))
    for g in range(summed // 2, (summed + relayed) // 2):
        ends.append((max(n for link in (LOW, HIGH) for (_, c), n in at[link].items() if c in (2 * g, 2 * g + 1)), g))
    return [(min(n, last), g) for n, g in sorted(ends)]


def kernel(
    group_count,
    beta_list_hbm,
    beta_kind_hbm,
    opp_beta_kind_hbm,
    alpha_list_hbm,
    alpha_kind_hbm,
    opp_list_hbm,
    opp_kind_hbm,
    coeffs_hbm,
    beta_table_hbm,
    alpha_table_hbm,
    opp_alpha_table_hbm,
    opp_beta_table_hbm,
    out,
    beta_list,
    beta_kind,
    opp_beta_kind,
    alpha_list,
    alpha_kind,
    opp_list,
    opp_kind,
    coeffs,
    tables,
    plane,
    cross,
    sums,
    staged,
    passing,
    whole,
    half,
    acc,
    mine,
    tiles,
    onward,
    load_sem,
    own_send,
    plane_recv,
    relay_send,
    z_send,
    cross_recv,
    sum_send,
    pass_send,
    pass_recv,
    forward_send,
    hop_send,
    pair_send,
    pair_recv,
    half_send,
    half_recv,
):
    rows, cols = coeffs.shape
    kinds, tile = tables.shape[1:3]
    count = cols // tile
    relayed = count // 2
    summed = count - relayed
    plans = make_plans(summed, relayed)
    slots, _ = slots_of(plans)
    beta_table, alpha_table, opp_alpha_table, opp_beta_table = (tables.at[k] for k in range(4))
    me, core = lax.axis_index("alpha"), lax.axis_index("beta")
    z, p = me // GROUP, me % GROUP
    x, y = p % 2, p // 2
    places = (p + 1 - 2 * x, p + 2 - 4 * y, 3 - p)
    mates = tuple(z * GROUP + q for q in places)
    steps = (1 - 2 * x, 1 - 2 * y, 1 - 2 * y)
    middle = x + y == 1
    corner = jnp.logical_not(middle)

    def inside(group):
        return (group >= 0) & (group < group_count)

    has_out = [inside(z + step) for step in steps]
    has_in = [inside(z - step) for step in steps]

    def chip(index):
        return (index, core)

    pair = (me, 1 - core)

    def send(src, dst, send_sem, recv_sem, device):
        return pltpu.make_async_remote_copy(
            src_ref=src,
            dst_ref=dst,
            send_sem=send_sem,
            recv_sem=recv_sem,
            device_id=device,
            device_id_type=pl.DeviceIdType.MESH,
        )

    def sent(ref, sem):
        send(ref, ref, sem, sem, pair).wait_send()

    def arrived(ref, sem):
        send(ref, ref, sem, sem, pair).wait_recv()

    def columns(c):
        return pl.ds(c * tile, tile)

    def wide(g):
        return pl.ds(g * 2 * tile, 2 * tile)

    def both(g):
        return pl.ds(2 * g, 2)

    def own_copy(to, n, c):
        return send(
            coeffs.at[:, columns(c)],
            plane.at[to, c],
            own_send.at[to],
            plane_recv.at[to, slots[to][n]],
            chip(mates[to]),
        )

    def relay_copy(to, n, c):
        return send(
            plane.at[HIGH if to == LOW else LOW, c],
            plane.at[DIAG, c],
            relay_send,
            plane_recv.at[to, slots[to][n]],
            chip(mates[to]),
        )

    def z_copy(r, c):
        return send(
            plane.at[r, c],
            cross.at[r, c],
            z_send.at[r],
            cross_recv.at[min(r, 1), c // 2],
            chip(me + GROUP * steps[r]),
        )

    def sum_copy(c):
        return send(staged.at[c], sums.at[c], sum_send, cross_recv.at[0, c // 2], chip(me + GROUP * steps[LOW]))

    def pass_copy(c):
        k = c - summed
        return send(
            coeffs.at[:, columns(c)], passing.at[k], pass_send, pass_recv.at[k // 2], chip(me - GROUP * steps[HIGH])
        )

    def forward_copy(n, c):
        return send(
            passing.at[c - summed],
            cross.at[HIGH, c],
            forward_send,
            plane_recv.at[HIGH, slots[HIGH][n]],
            chip(mates[HIGH]),
        )

    def hop_copy(c):
        return send(cross.at[HIGH, c], cross.at[DIAG, c], hop_send, cross_recv.at[1, c // 2], chip(mates[LOW]))

    def half_copy(g):
        part = half.at[pl.ds(core * count + 2 * g, 2)]
        return send(part, part, half_send, half_recv, pair)

    def pair_copy(t):
        part = coeffs_hbm.at[:, pl.ds(t * tile, tile)]
        return send(part, whole.at[core * count + t], pair_send, pair_recv, pair)

    lists = (
        (alpha_list_hbm, alpha_list),
        (alpha_kind_hbm, alpha_kind),
        (opp_list_hbm, opp_list),
        (opp_kind_hbm, opp_kind),
        (beta_list_hbm, beta_list),
        (beta_kind_hbm, beta_kind),
        (opp_beta_kind_hbm, opp_beta_kind),
    )
    load_coeffs = pltpu.make_async_copy(coeffs_hbm, coeffs, load_sem.at[0])
    load_lists = [pltpu.make_async_copy(src, dst, load_sem.at[2 + k]) for k, (src, dst) in enumerate(lists)]
    load_coeffs.start()
    for load in load_lists:
        load.start()
    for k, src in enumerate((beta_table_hbm, alpha_table_hbm, opp_alpha_table_hbm, opp_beta_table_hbm)):
        pltpu.make_async_copy(src, tables.at[k], load_sem.at[1]).start()

    barrier = pltpu.get_barrier_semaphore()
    for device in (chip(mates[LOW]), chip(mates[HIGH]), pair):
        pl.semaphore_signal(barrier, inc=1, device_id=device, device_id_type=pl.DeviceIdType.MESH)
    up, down = inside(z + 1), inside(z - 1)
    for there, offset in ((up, GROUP), (down, -GROUP)):

        @pl.when(there)
        def _():
            pl.semaphore_signal(
                barrier, inc=1, device_id=chip(me + offset), device_id_type=pl.DeviceIdType.MESH
            )

    load_coeffs.wait()
    pl.semaphore_wait(barrier, 3 + up.astype(jnp.int32) + down.astype(jnp.int32))

    for n in range(AHEAD):
        for link in (LOW, HIGH):
            own_copy(link, n, plans[link][n][1]).start()

    @pl.when(has_in[HIGH])
    def _():
        for c in range(summed, count):
            pass_copy(c).start()

    for t in range(count):
        pair_copy(t).start()
    for load in load_lists:
        load.wait()
    pltpu.make_async_copy(tables, tables, load_sem.at[1]).wait()

    for t in range(count):
        whole[core * count + t] = coeffs[:, t * tile : (t + 1) * tile]

    for r in range(3):

        @pl.when(jnp.logical_not(has_in[r]))
        def _():
            cross[r] = jnp.zeros_like(cross[r])

    @pl.when(corner & jnp.logical_not(has_in[LOW]))
    def _():
        sums[...] = jnp.zeros_like(sums)

    sources = [me, *mates] + [mates[r] - GROUP * steps[r] for r in range(3)]
    for slot, source in enumerate(sources):
        at = pl.ds(slot * tile, tile)
        tiles[:tile, at] = picked_tile(me, alpha_list, alpha_kind, alpha_table, source).astype(BF16)
        tiles[tile:, at] = picked_tile(me, opp_list, opp_kind, opp_alpha_table, source).astype(BF16)

    summing = corner & has_out[LOW]

    @pl.when(summing)
    def _():
        target = me + GROUP * steps[LOW]
        for slot, source in enumerate(mates):
            at = pl.ds(slot * tile, tile)
            onward[:tile, at] = picked_tile(target, alpha_list, alpha_kind, alpha_table, source).astype(BF16)
            onward[tile:, at] = picked_tile(target, opp_list, opp_kind, opp_alpha_table, source).astype(BF16)

    def product(weights, first, blocks):
        return jnp.dot(
            weights[:, first * tile : (first + len(blocks)) * tile],
            jnp.concatenate(blocks, axis=0),
            preferred_element_type=F32,
        )

    def wide_block(ref, r, g):
        return jnp.concatenate([ref[r, 2 * g], ref[r, 2 * g + 1]], axis=1)

    def beta_apply(data, kind, table, j):
        left, right = [], []
        for link in range(beta_list.shape[0]):
            left.append(data[beta_list[link, j]])
            right.append(table[kind[link, j]])
        return lax.dot_general(
            jnp.concatenate(left, axis=1),
            jnp.concatenate(right, axis=1),
            (((1,), (1,)), ((), ())),
            preferred_element_type=F32,
        )

    def same_spin(j):
        mine[:, columns(j)] = beta_apply(whole, beta_kind, beta_table, j)

    def in_plane(g):
        acc[:, wide(g)] = product(
            tiles, 0, [coeffs[:, wide(g)], *(wide_block(plane, r, g) for r in range(3))]
        )

    def cross_wait(first, g, there=True):
        @pl.when(has_in[first] & there)
        def _():
            if first == LOW or 2 * g >= summed:
                arrived(cross.at[LOW if first == LOW else DIAG, both(g)], cross_recv.at[first, g])
            else:
                arrived(cross.at[pl.ds(HIGH, 2), both(g)], cross_recv.at[first, g])

    def settle(g, added):
        total = added
        for t in range(2):
            half[core * count + 2 * g + t] = total[tile:, t * tile : (t + 1) * tile].astype(BF16)
        mine[:, wide(g)] += total[:tile]

    def close(g):
        there = True if 2 * g >= summed else middle
        cross_wait(LOW, g, there)
        cross_wait(HIGH, g, there)
        if 2 * g < summed:

            @pl.when(corner & has_in[LOW])
            def _():
                arrived(sums.at[both(g)], cross_recv.at[0, g])

        if 2 * g >= summed:
            settle(
                g,
                product(
                    tiles,
                    0,
                    [
                        coeffs[:, wide(g)],
                        *(wide_block(plane, r, g) for r in range(3)),
                        *(wide_block(cross, r, g) for r in range(3)),
                    ],
                ),
            )
        else:

            @pl.when(middle)
            def _():
                settle(g, acc[:, wide(g)] + product(tiles, 4, [wide_block(cross, r, g) for r in range(3)]))

            @pl.when(corner)
            def _():
                settle(g, acc[:, wide(g)] + jnp.concatenate([sums[2 * g], sums[2 * g + 1]], axis=1).astype(F32))

        half_copy(g).start()

    def sum_up(g):
        @pl.when(summing)
        def _():
            found = product(onward, 0, [wide_block(plane, r, g) for r in range(3)]).astype(BF16)
            for t in range(2):
                staged[2 * g + t] = found[:, t * tile : (t + 1) * tile]
                sum_copy(2 * g + t).start()

    seen = set()

    def take(link, n):
        kind, c = plans[link][n]
        if kind == "o":
            own_copy(link, n, c).wait_recv()
            if link == LOW:
                there = has_out[LOW] if c >= summed else has_out[LOW] & middle
            else:
                there = has_out[HIGH] & middle
            if link == LOW or c < summed:

                @pl.when(there)
                def _():
                    z_copy(link, c).start()

        elif kind == "r":
            relay_copy(link, n, c).wait_recv()

            @pl.when(middle & has_out[DIAG])
            def _():
                z_copy(DIAG, c).start()

            seen.add(c)
            if c < summed and c ^ 1 in seen:
                sum_up(c // 2)
                in_plane(c // 2)
        elif kind == "f":

            @pl.when(has_in[HIGH])
            def _():
                forward_copy(n, c).wait_recv()

    def issue(link, n):
        kind, c = plans[link][n]
        if kind == "o":
            own_copy(link, n, c).start()
        elif kind == "r":
            relay_copy(link, n, c).start()
        elif kind == "f":

            @pl.when(has_out[HIGH])
            def _():
                if c % 2 == 0:
                    k = c - summed
                    arrived(passing.at[pl.ds(k, 2)], pass_recv.at[k // 2])
                forward_copy(n, c).start()

        elif kind == "h":

            @pl.when(middle & has_in[HIGH])
            def _():
                hop_copy(c).start()

    last = len(plans[LOW])
    after = {i: [] for i in range(-1, last)}

    def put(i, what, *args):
        after[i].append((what, args))

    for j in range(count):
        put(-1, same_spin, j)
    for n, g in closing(plans, summed, relayed):
        put(n, close, g)

    arrived(whole.at[pl.ds((1 - core) * count, count)], pair_recv)
    for i in range(-1, last):
        if i >= 0:
            for link in (LOW, HIGH):
                take(link, i)
            if i + AHEAD < last:
                for link in (LOW, HIGH):
                    issue(link, i + AHEAD)
        for what, args in after[i]:
            what(*args)

    arrived(half.at[pl.ds((1 - core) * count, count)], half_recv)
    for j in range(count):
        mixed = beta_apply(half, opp_beta_kind, opp_beta_table, j)
        out[:, columns(j)] = (mine[:, columns(j)] + mixed).astype(BF16)

    sent(coeffs, own_send.at[LOW])
    sent(coeffs, own_send.at[HIGH])
    sent(whole.at[pl.ds(0, count)], pair_send)
    sent(half.at[pl.ds(0, count)], half_send)
    sent(plane.at[DIAG], relay_send)

    @pl.when(has_in[HIGH])
    def _():
        sent(passing, pass_send)

    @pl.when(has_out[HIGH])
    def _():
        sent(passing, forward_send)

    @pl.when(middle & has_in[HIGH])
    def _():
        sent(passing, hop_send)

    @pl.when(middle & has_out[LOW])
    def _():
        sent(plane.at[LOW], z_send.at[LOW])

    @pl.when(middle & has_out[HIGH])
    def _():
        sent(plane.at[HIGH, pl.ds(0, summed)], z_send.at[HIGH])
        sent(plane.at[DIAG], z_send.at[DIAG])

    @pl.when(summing)
    def _():
        sent(plane.at[LOW, pl.ds(0, relayed)], z_send.at[LOW])
        sent(staged, sum_send)


def local(group_count, coeffs, *rest):
    lists, tables = rest[:7], rest[7:]
    flat = coeffs.reshape(coeffs.shape[1:])
    rows, cols = flat.shape
    kinds, tile = tables[0].shape[:2]
    count = cols // tile
    relayed, groups = count // 2, count // 2
    summed = count - relayed
    operands = tuple(
        pltpu.with_memory_space_constraint(one, pltpu.HBM) for one in (*(one.T for one in lists), flat, *tables)
    )
    in_lists = [pltpu.SMEM(one.shape, one.dtype) for one in operands[:7]]
    dma = pltpu.SemaphoreType.DMA
    result = pl.pallas_call(
        functools.partial(kernel, group_count),
        out_shape=jax.ShapeDtypeStruct((rows, cols), BF16),
        in_specs=[pl.BlockSpec(memory_space=pltpu.HBM)] * len(operands),
        out_specs=pl.BlockSpec(memory_space=pltpu.VMEM),
        scratch_shapes=[
            *in_lists,
            pltpu.VMEM((rows, cols), BF16),
            pltpu.VMEM((len(tables), *tables[0].shape), BF16),
            pltpu.VMEM((3, count, rows, tile), BF16),
            pltpu.VMEM((3, count, rows, tile), BF16),
            pltpu.VMEM((summed, 2 * rows, tile), BF16),
            pltpu.VMEM((summed, 2 * rows, tile), BF16),
            pltpu.VMEM((relayed, rows, tile), BF16),
            pltpu.VMEM((2 * count, rows, tile), BF16),
            pltpu.VMEM((2 * count, rows, tile), BF16),
            pltpu.VMEM((2 * tile, cols), F32),
            pltpu.VMEM((rows, cols), F32),
            pltpu.VMEM((2 * tile, 7 * tile), BF16),
            pltpu.VMEM((2 * tile, 3 * tile), BF16),
            dma((9,)),
            dma((2,)),
            dma((2, slots_of(make_plans(summed, relayed))[1])),
            dma,
            dma((3,)),
            dma((2, groups)),
            dma,
            dma,
            dma((relayed // 2,)),
            dma,
            dma,
            dma,
            dma,
            dma,
            dma,
        ],
        compiler_params=pltpu.CompilerParams(
            collective_id=0, has_side_effects=True, vmem_limit_bytes=20000 * 1024
        ),
    )(*operands)
    return result.reshape(coeffs.shape)


def solution(mesh):
    halves = P("beta", None)
    return jax.shard_map(
        functools.partial(local, mesh.shape["alpha"] // GROUP),
        mesh=mesh,
        in_specs=(P(None, "alpha", "beta"), halves, halves, halves) + (P(),) * 8,
        out_specs=P(None, "alpha", "beta"),
        check_vma=False,
    )
```

```python
import functools

import jax
import jax.numpy as jnp
from jax import lax
from jax.experimental import pallas as pl
from jax.experimental.pallas import tpu as pltpu
from jax.sharding import PartitionSpec as P

GROUP = 4
AHEAD = 6
FORWARD, STRIDE = 15, 7
DELAY = 3
SHIFT = 3
OPEN = (7, 5)
BF16, F32 = jnp.bfloat16, jnp.float32
LOW, HIGH, DIAG = range(3)


def picked_tile(block, lists, kinds, table, source):
    kind, found = jnp.int32(0), jnp.int32(0)
    for link in range(lists.shape[0]):
        hit = (lists[link, block] == source).astype(jnp.int32)
        kind += hit * kinds[link, block]
        found += hit
    return table[kind].astype(F32) * found.astype(F32)


def order_of(summed, relayed):
    spread = [(2 * g + 1, summed, "s", g) for g in range(summed // 2)]
    spread += [(2 * g + SHIFT, relayed, "r", g) for g in range(relayed // 2)]
    return [(kind, g) for _, _, kind, g in sorted(spread, key=lambda one: one[0] / one[1])]


def make_plans(summed, relayed):
    wanted = {LOW: [], HIGH: []}
    for kind, g in order_of(summed, relayed):
        first = 2 * g + (summed if kind == "r" else 0)
        wanted[LOW] += [first, first + 1]
        wanted[HIGH] += [first + 1, first]
    late = [c for c in wanted[HIGH] if c >= summed and c % 2 == 0]
    own = {LOW: list(wanted[LOW]), HIGH: [c for c in wanted[HIGH] if c not in late] + late}
    relays = {LOW: [c for c in wanted[HIGH] if c % 2 == 1], HIGH: [c for c in wanted[LOW] if c % 2 == 0]}
    plans, own_at, forward_at = ([], []), ({}, {}), []
    passed = hopped = n = 0
    while own[LOW] or own[HIGH] or relays[LOW] or relays[HIGH] or hopped < relayed:
        for link in (LOW, HIGH):
            other = HIGH if link == LOW else LOW
            due = passed < relayed and n >= FORWARD + STRIDE * passed // 4
            ready = relays[link] and own_at[other].get(relays[link][0], n) + AHEAD <= n
            spare = not own[link] or own[link][0] in late
            if ready:
                plans[link].append(("r", relays[link].pop(0)))
            elif link == HIGH and passed < relayed and (due or spare):
                plans[link].append(("f", summed + passed))
                forward_at.append(n)
                passed += 1
            elif own[link]:
                own_at[link][own[link][0]] = n
                plans[link].append(("o", own[link].pop(0)))
            elif link == LOW and hopped < passed and forward_at[hopped] + AHEAD <= n:
                plans[link].append(("h", summed + hopped))
                hopped += 1
            else:
                plans[link].append((None, None))
        n += 1
    return plans


def issue_times(plans):
    times = []
    for most in OPEN:
        per_link = ([], [])
        for link, plan in enumerate(plans):
            for n, (kind, c) in enumerate(plan):
                need = {"r": ("o", c), "h": ("f", c)}.get(kind)
                after = found_on(plans, 1 - link, need) if need else -1
                per_link[link].append(max([n - most, after, -1, *per_link[link][-1:]]))
        times.append(per_link)
    return times


def found_on(plans, link, item):
    return plans[link].index(item)


def slots_of(plans):
    times, slots, most = issue_times(plans), ([], []), 0
    for link, plan in enumerate(plans):
        held = []
        for n, (kind, _) in enumerate(plan):
            free = len(plan)
            for when in times:
                sure = [k for k in range(when[link][n] + 1) if plan[k][0] in ("o", "r")]
                free = min(free, when[link][sure[-1]] if sure else -1)
            if kind in ("o", "r", "f"):
                spot = next((k for k, user in enumerate(held) if user <= free), len(held))
                held[spot : spot + 1] = [n]
                slots[link].append(spot)
            else:
                slots[link].append(None)
        most = max(most, len(held))
    return slots, most


def closing(plans, summed, relayed):
    at = [{item: n for n, item in enumerate(plan)} for plan in plans]
    last = len(plans[LOW]) - 1
    free, ends = 0, []
    events = [(n, c) for (kind, c), n in at[LOW].items() if kind == "o" and c >= summed]
    for g in range(summed // 2):
        events.append((max(at[LOW]["r", 2 * g + 1], at[HIGH]["r", 2 * g]), 2 * g))
    for n, c in sorted(events):
        free = max(free, n) + (1 if c >= summed else 4)
        if c < summed:
            ends.append((free + DELAY, c // 2))
    for g in range(summed // 2, (summed + relayed) // 2):
        ends.append((max(n for link in (LOW, HIGH) for (_, c), n in at[link].items() if c in (2 * g, 2 * g + 1)), g))
    return [(min(n, last), g) for n, g in sorted(ends)]


def kernel(
    group_count,
    beta_list_hbm,
    beta_kind_hbm,
    opp_beta_kind_hbm,
    alpha_list_hbm,
    alpha_kind_hbm,
    opp_list_hbm,
    opp_kind_hbm,
    coeffs_hbm,
    beta_table_hbm,
    alpha_table_hbm,
    opp_alpha_table_hbm,
    opp_beta_table_hbm,
    out,
    beta_list,
    beta_kind,
    opp_beta_kind,
    alpha_list,
    alpha_kind,
    opp_list,
    opp_kind,
    coeffs,
    tables,
    plane,
    cross,
    sums,
    staged,
    passing,
    whole,
    half,
    acc,
    mine,
    tiles,
    onward,
    load_sem,
    own_send,
    plane_recv,
    relay_send,
    z_send,
    cross_recv,
    sum_send,
    pass_send,
    pass_recv,
    forward_send,
    hop_send,
    pair_send,
    pair_recv,
    half_send,
    half_recv,
):
    rows, cols = coeffs.shape
    kinds, tile = tables.shape[1:3]
    count = cols // tile
    relayed = count // 2
    summed = count - relayed
    plans = make_plans(summed, relayed)
    slots, _ = slots_of(plans)
    beta_table, alpha_table, opp_alpha_table, opp_beta_table = (tables.at[k] for k in range(4))
    me, core = lax.axis_index("alpha"), lax.axis_index("beta")
    z, p = me // GROUP, me % GROUP
    x, y = p % 2, p // 2
    places = (p + 1 - 2 * x, p + 2 - 4 * y, 3 - p)
    mates = tuple(z * GROUP + q for q in places)
    steps = (1 - 2 * x, 1 - 2 * y, 1 - 2 * y)
    middle = x + y == 1
    corner = jnp.logical_not(middle)

    def inside(group):
        return (group >= 0) & (group < group_count)

    has_out = [inside(z + step) for step in steps]
    has_in = [inside(z - step) for step in steps]

    def chip(index):
        return (index, core)

    pair = (me, 1 - core)

    def send(src, dst, send_sem, recv_sem, device):
        return pltpu.make_async_remote_copy(
            src_ref=src,
            dst_ref=dst,
            send_sem=send_sem,
            recv_sem=recv_sem,
            device_id=device,
            device_id_type=pl.DeviceIdType.MESH,
        )

    def sent(ref, sem):
        send(ref, ref, sem, sem, pair).wait_send()

    def arrived(ref, sem):
        send(ref, ref, sem, sem, pair).wait_recv()

    def columns(c):
        return pl.ds(c * tile, tile)

    def wide(g):
        return pl.ds(g * 2 * tile, 2 * tile)

    def both(g):
        return pl.ds(2 * g, 2)

    def own_copy(to, n, c):
        return send(
            coeffs.at[:, columns(c)],
            plane.at[to, c],
            own_send.at[to],
            plane_recv.at[to, slots[to][n]],
            chip(mates[to]),
        )

    def relay_copy(to, n, c):
        return send(
            plane.at[HIGH if to == LOW else LOW, c],
            plane.at[DIAG, c],
            relay_send,
            plane_recv.at[to, slots[to][n]],
            chip(mates[to]),
        )

    def z_copy(r, c):
        return send(
            plane.at[r, c],
            cross.at[r, c],
            z_send.at[r],
            cross_recv.at[min(r, 1), c // 2],
            chip(me + GROUP * steps[r]),
        )

    def sum_copy(c):
        return send(staged.at[c], sums.at[c], sum_send, cross_recv.at[0, c // 2], chip(me + GROUP * steps[LOW]))

    def pass_copy(c):
        k = c - summed
        return send(
            coeffs.at[:, columns(c)], passing.at[k], pass_send, pass_recv.at[k // 2], chip(me - GROUP * steps[HIGH])
        )

    def forward_copy(n, c):
        return send(
            passing.at[c - summed],
            cross.at[HIGH, c],
            forward_send,
            plane_recv.at[HIGH, slots[HIGH][n]],
            chip(mates[HIGH]),
        )

    def hop_copy(c):
        return send(cross.at[HIGH, c], cross.at[DIAG, c], hop_send, cross_recv.at[1, c // 2], chip(mates[LOW]))

    def half_copy(g):
        part = half.at[pl.ds(core * count + 2 * g, 2)]
        return send(part, part, half_send, half_recv, pair)

    def pair_copy(t):
        part = coeffs_hbm.at[:, pl.ds(t * tile, tile)]
        return send(part, whole.at[core * count + t], pair_send, pair_recv, pair)

    lists = (
        (alpha_list_hbm, alpha_list),
        (alpha_kind_hbm, alpha_kind),
        (opp_list_hbm, opp_list),
        (opp_kind_hbm, opp_kind),
        (beta_list_hbm, beta_list),
        (beta_kind_hbm, beta_kind),
        (opp_beta_kind_hbm, opp_beta_kind),
    )
    load_coeffs = pltpu.make_async_copy(coeffs_hbm, coeffs, load_sem.at[0])
    load_lists = [pltpu.make_async_copy(src, dst, load_sem.at[2 + k]) for k, (src, dst) in enumerate(lists)]
    load_coeffs.start()
    for load in load_lists:
        load.start()
    for k, src in enumerate((beta_table_hbm, alpha_table_hbm, opp_alpha_table_hbm, opp_beta_table_hbm)):
        pltpu.make_async_copy(src, tables.at[k], load_sem.at[1]).start()

    barrier = pltpu.get_barrier_semaphore()
    for device in (chip(mates[LOW]), chip(mates[HIGH]), pair):
        pl.semaphore_signal(barrier, inc=1, device_id=device, device_id_type=pl.DeviceIdType.MESH)
    up, down = inside(z + 1), inside(z - 1)
    for there, offset in ((up, GROUP), (down, -GROUP)):

        @pl.when(there)
        def _():
            pl.semaphore_signal(
                barrier, inc=1, device_id=chip(me + offset), device_id_type=pl.DeviceIdType.MESH
            )

    load_coeffs.wait()
    pl.semaphore_wait(barrier, 3 + up.astype(jnp.int32) + down.astype(jnp.int32))

    def issue(link, n):
        kind, c = plans[link][n]
        if kind == "o":
            own_copy(link, n, c).start()
        elif kind == "r":
            relay_copy(link, n, c).start()
        elif kind == "f":

            @pl.when(has_out[HIGH])
            def _():
                if c % 2 == 0:
                    k = c - summed
                    arrived(passing.at[pl.ds(k, 2)], pass_recv.at[k // 2])
                forward_copy(n, c).start()

        elif kind == "h":

            @pl.when(middle & has_in[HIGH])
            def _():
                hop_copy(c).start()

    times = issue_times(plans)

    def issue_after(i):
        due = [[(link, n) for n in range(last) for link in (LOW, HIGH) if when[link][n] == i] for when in times]
        if due[0] == due[1]:
            for link, n in due[0]:
                issue(link, n)
        else:
            for which in range(2):

                @pl.when(core == which)
                def _():
                    for link, n in due[which]:
                        issue(link, n)

    last = len(plans[LOW])
    issue_after(-1)

    @pl.when(has_in[HIGH])
    def _():
        for c in range(summed, count):
            pass_copy(c).start()

    for t in range(count):
        pair_copy(t).start()
    for load in load_lists:
        load.wait()
    pltpu.make_async_copy(tables, tables, load_sem.at[1]).wait()

    for t in range(count):
        whole[core * count + t] = coeffs[:, t * tile : (t + 1) * tile]

    for r in range(3):

        @pl.when(jnp.logical_not(has_in[r]))
        def _():
            cross[r] = jnp.zeros_like(cross[r])

    @pl.when(corner & jnp.logical_not(has_in[LOW]))
    def _():
        sums[...] = jnp.zeros_like(sums)

    sources = [me, mates[LOW], mates[DIAG], mates[HIGH]] + [mates[r] - GROUP * steps[r] for r in range(3)]
    for slot, source in enumerate(sources):
        at = pl.ds(slot * tile, tile)
        tiles[:tile, at] = picked_tile(me, alpha_list, alpha_kind, alpha_table, source).astype(BF16)
        tiles[tile:, at] = picked_tile(me, opp_list, opp_kind, opp_alpha_table, source).astype(BF16)

    summing = corner & has_out[LOW]

    @pl.when(summing)
    def _():
        target = me + GROUP * steps[LOW]
        for slot, source in enumerate(mates):
            at = pl.ds(slot * tile, tile)
            onward[:tile, at] = picked_tile(target, alpha_list, alpha_kind, alpha_table, source).astype(BF16)
            onward[tile:, at] = picked_tile(target, opp_list, opp_kind, opp_alpha_table, source).astype(BF16)

    def product(weights, first, blocks):
        return jnp.dot(
            weights[:, first * tile : (first + len(blocks)) * tile],
            jnp.concatenate(blocks, axis=0),
            preferred_element_type=F32,
        )

    def wide_block(ref, r, g):
        return jnp.concatenate([ref[r, 2 * g], ref[r, 2 * g + 1]], axis=1)

    def beta_apply(data, kind, table, j):
        left, right = [], []
        for link in range(beta_list.shape[0]):
            left.append(data[beta_list[link, j]])
            right.append(table[kind[link, j]])
        return lax.dot_general(
            jnp.concatenate(left, axis=1),
            jnp.concatenate(right, axis=1),
            (((1,), (1,)), ((), ())),
            preferred_element_type=F32,
        )

    def same_spin(j):
        mine[:, columns(j)] = beta_apply(whole, beta_kind, beta_table, j)

    def in_plane(g):
        blocks = [coeffs[:, wide(g)], wide_block(plane, LOW, g), wide_block(plane, DIAG, g)]
        if 2 * g < summed:
            blocks.append(wide_block(plane, HIGH, g))
        acc[:, wide(g)] = product(tiles, 0, blocks)

    def cross_wait(first, g, there=True):
        @pl.when(has_in[first] & there)
        def _():
            if first == LOW or 2 * g >= summed:
                arrived(cross.at[LOW if first == LOW else DIAG, both(g)], cross_recv.at[first, g])
            else:
                arrived(cross.at[pl.ds(HIGH, 2), both(g)], cross_recv.at[first, g])

    def settle(g, added):
        total = added
        for t in range(2):
            half[core * count + 2 * g + t] = total[tile:, t * tile : (t + 1) * tile].astype(BF16)
        mine[:, wide(g)] += total[:tile]

    def close(g):
        there = True if 2 * g >= summed else middle
        cross_wait(LOW, g, there)
        cross_wait(HIGH, g, there)
        if 2 * g < summed:

            @pl.when(corner & has_in[LOW])
            def _():
                arrived(sums.at[both(g)], cross_recv.at[0, g])

        if 2 * g >= summed:
            blocks = [wide_block(plane, HIGH, g), *(wide_block(cross, r, g) for r in range(3))]
            settle(g, acc[:, wide(g)] + product(tiles, 3, blocks))
        else:

            @pl.when(middle)
            def _():
                settle(g, acc[:, wide(g)] + product(tiles, 4, [wide_block(cross, r, g) for r in range(3)]))

            @pl.when(corner)
            def _():
                settle(g, acc[:, wide(g)] + jnp.concatenate([sums[2 * g], sums[2 * g + 1]], axis=1).astype(F32))

        half_copy(g).start()

    def sum_up(g):
        @pl.when(summing)
        def _():
            found = product(onward, 0, [wide_block(plane, r, g) for r in range(3)]).astype(BF16)
            for t in range(2):
                staged[2 * g + t] = found[:, t * tile : (t + 1) * tile]
                sum_copy(2 * g + t).start()

    seen = set()

    def take(link, n):
        kind, c = plans[link][n]
        if kind == "o":
            own_copy(link, n, c).wait_recv()
            if link == LOW:
                there = has_out[LOW] if c >= summed else has_out[LOW] & middle
            else:
                there = has_out[HIGH] & middle
            if link == LOW or c < summed:

                @pl.when(there)
                def _():
                    z_copy(link, c).start()

        elif kind == "r":
            relay_copy(link, n, c).wait_recv()

            @pl.when(middle & has_out[DIAG])
            def _():
                z_copy(DIAG, c).start()

            seen.add(c)
            if c ^ 1 in seen:
                if c < summed:
                    sum_up(c // 2)
                in_plane(c // 2)
        elif kind == "f":

            @pl.when(has_in[HIGH])
            def _():
                forward_copy(n, c).wait_recv()

    after = {i: [] for i in range(-1, last)}

    def put(i, what, *args):
        after[i].append((what, args))

    for j in range(count):
        put(-1, same_spin, j)
    for n, g in closing(plans, summed, relayed):
        put(n, close, g)

    arrived(whole.at[pl.ds((1 - core) * count, count)], pair_recv)
    for i in range(-1, last):
        if i >= 0:
            for link in (LOW, HIGH):
                take(link, i)
            issue_after(i)
        for what, args in after[i]:
            what(*args)

    arrived(half.at[pl.ds((1 - core) * count, count)], half_recv)
    for j in range(count):
        mixed = beta_apply(half, opp_beta_kind, opp_beta_table, j)
        out[:, columns(j)] = (mine[:, columns(j)] + mixed).astype(BF16)

    sent(coeffs, own_send.at[LOW])
    sent(coeffs, own_send.at[HIGH])
    sent(whole.at[pl.ds(0, count)], pair_send)
    sent(half.at[pl.ds(0, count)], half_send)
    sent(plane.at[DIAG], relay_send)

    @pl.when(has_in[HIGH])
    def _():
        sent(passing, pass_send)

    @pl.when(has_out[HIGH])
    def _():
        sent(passing, forward_send)

    @pl.when(middle & has_in[HIGH])
    def _():
        sent(passing, hop_send)

    @pl.when(middle & has_out[LOW])
    def _():
        sent(plane.at[LOW], z_send.at[LOW])

    @pl.when(middle & has_out[HIGH])
    def _():
        sent(plane.at[HIGH, pl.ds(0, summed)], z_send.at[HIGH])
        sent(plane.at[DIAG], z_send.at[DIAG])

    @pl.when(summing)
    def _():
        sent(plane.at[LOW, pl.ds(0, relayed)], z_send.at[LOW])
        sent(staged, sum_send)


def local(group_count, coeffs, *rest):
    lists, tables = rest[:7], rest[7:]
    flat = coeffs.reshape(coeffs.shape[1:])
    rows, cols = flat.shape
    kinds, tile = tables[0].shape[:2]
    count = cols // tile
    relayed, groups = count // 2, count // 2
    summed = count - relayed
    operands = tuple(
        pltpu.with_memory_space_constraint(one, pltpu.HBM) for one in (*(one.T for one in lists), flat, *tables)
    )
    in_lists = [pltpu.SMEM(one.shape, one.dtype) for one in operands[:7]]
    dma = pltpu.SemaphoreType.DMA
    result = pl.pallas_call(
        functools.partial(kernel, group_count),
        out_shape=jax.ShapeDtypeStruct((rows, cols), BF16),
        in_specs=[pl.BlockSpec(memory_space=pltpu.HBM)] * len(operands),
        out_specs=pl.BlockSpec(memory_space=pltpu.VMEM),
        scratch_shapes=[
            *in_lists,
            pltpu.VMEM((rows, cols), BF16),
            pltpu.VMEM((len(tables), *tables[0].shape), BF16),
            pltpu.VMEM((3, count, rows, tile), BF16),
            pltpu.VMEM((3, count, rows, tile), BF16),
            pltpu.VMEM((summed, 2 * rows, tile), BF16),
            pltpu.VMEM((summed, 2 * rows, tile), BF16),
            pltpu.VMEM((relayed, rows, tile), BF16),
            pltpu.VMEM((2 * count, rows, tile), BF16),
            pltpu.VMEM((2 * count, rows, tile), BF16),
            pltpu.VMEM((2 * tile, cols), F32),
            pltpu.VMEM((rows, cols), F32),
            pltpu.VMEM((2 * tile, 7 * tile), BF16),
            pltpu.VMEM((2 * tile, 3 * tile), BF16),
            dma((9,)),
            dma((2,)),
            dma((2, slots_of(make_plans(summed, relayed))[1])),
            dma,
            dma((3,)),
            dma((2, groups)),
            dma,
            dma,
            dma((relayed // 2,)),
            dma,
            dma,
            dma,
            dma,
            dma,
            dma,
        ],
        compiler_params=pltpu.CompilerParams(
            collective_id=0, has_side_effects=True, vmem_limit_bytes=20000 * 1024
        ),
    )(*operands)
    return result.reshape(coeffs.shape)


def solution(mesh):
    halves = P("beta", None)
    return jax.shard_map(
        functools.partial(local, mesh.shape["alpha"] // GROUP),
        mesh=mesh,
        in_specs=(P(None, "alpha", "beta"), halves, halves, halves) + (P(),) * 8,
        out_specs=P(None, "alpha", "beta"),
        check_vma=False,
    )
```

```python
import functools

import jax
import jax.numpy as jnp
from jax import lax
from jax.experimental import pallas as pl
from jax.experimental.pallas import tpu as pltpu
from jax.sharding import PartitionSpec as P

GROUP = 4
AHEAD = 6
FORWARD, STRIDE = 15, 7
DELAY = 4
SHIFT = 3
OPEN = (7, 5)
BF16, F32 = jnp.bfloat16, jnp.float32
LOW, HIGH, DIAG = range(3)


def picked_tile(block, lists, kinds, table, source):
    kind, found = jnp.int32(0), jnp.int32(0)
    for link in range(lists.shape[0]):
        hit = (lists[link, block] == source).astype(jnp.int32)
        kind += hit * kinds[link, block]
        found += hit
    return table[kind].astype(F32) * found.astype(F32)


def order_of(summed, relayed):
    spread = [(2 * g + 1, summed, "s", g) for g in range(summed // 2)]
    spread += [(2 * g + SHIFT, relayed, "r", g) for g in range(relayed // 2)]
    return [(kind, g) for _, _, kind, g in sorted(spread, key=lambda one: one[0] / one[1])]


def make_plans(summed, relayed):
    wanted = {LOW: [], HIGH: []}
    for kind, g in order_of(summed, relayed):
        first = 2 * g + (summed if kind == "r" else 0)
        wanted[LOW] += [first, first + 1]
        wanted[HIGH] += [first + 1, first]
    late = [c for c in wanted[HIGH] if c >= summed and c % 2 == 0]
    own = {LOW: list(wanted[LOW]), HIGH: [c for c in wanted[HIGH] if c not in late] + late}
    relays = {LOW: [c for c in wanted[HIGH] if c % 2 == 1], HIGH: [c for c in wanted[LOW] if c % 2 == 0]}
    plans, own_at, forward_at = ([], []), ({}, {}), []
    passed = hopped = n = 0
    while own[LOW] or own[HIGH] or relays[LOW] or relays[HIGH] or hopped < relayed:
        for link in (LOW, HIGH):
            other = HIGH if link == LOW else LOW
            due = passed < relayed and n >= FORWARD + STRIDE * passed // 4
            ready = relays[link] and own_at[other].get(relays[link][0], n) + AHEAD <= n
            spare = not own[link] or own[link][0] in late
            if ready:
                plans[link].append(("r", relays[link].pop(0)))
            elif link == HIGH and passed < relayed and (due or spare):
                plans[link].append(("f", summed + passed))
                forward_at.append(n)
                passed += 1
            elif own[link]:
                own_at[link][own[link][0]] = n
                plans[link].append(("o", own[link].pop(0)))
            elif link == LOW and hopped < passed and forward_at[hopped] + AHEAD <= n:
                plans[link].append(("h", summed + hopped))
                hopped += 1
            else:
                plans[link].append((None, None))
        n += 1
    return plans


def issue_times(plans):
    times = []
    for most in OPEN:
        per_link = ([], [])
        for link, plan in enumerate(plans):
            for n, (kind, c) in enumerate(plan):
                need = {"r": ("o", c), "h": ("f", c)}.get(kind)
                after = found_on(plans, 1 - link, need) if need else -1
                per_link[link].append(max([n - most, after, -1, *per_link[link][-1:]]))
        times.append(per_link)
    return times


def found_on(plans, link, item):
    return plans[link].index(item)


def slots_of(plans):
    times, slots, most = issue_times(plans), ([], []), 0
    for link, plan in enumerate(plans):
        held = []
        for n, (kind, _) in enumerate(plan):
            free = len(plan)
            for when in times:
                sure = [k for k in range(when[link][n] + 1) if plan[k][0] in ("o", "r")]
                free = min(free, when[link][sure[-1]] if sure else -1)
            if kind in ("o", "r", "f"):
                spot = next((k for k, user in enumerate(held) if user <= free), len(held))
                held[spot : spot + 1] = [n]
                slots[link].append(spot)
            else:
                slots[link].append(None)
        most = max(most, len(held))
    return slots, most


def closing(plans, summed, relayed):
    at = [{item: n for n, item in enumerate(plan)} for plan in plans]
    last = len(plans[LOW]) - 1
    free, ends = 0, []
    events = [(n, c) for (kind, c), n in at[LOW].items() if kind == "o" and c >= summed]
    for g in range(summed // 2):
        events.append((max(at[LOW]["r", 2 * g + 1], at[HIGH]["r", 2 * g]), 2 * g))
    for n, c in sorted(events):
        free = max(free, n) + (1 if c >= summed else 4)
        if c < summed:
            ends.append((free + DELAY, c // 2))
    for g in range(summed // 2, (summed + relayed) // 2):
        ends.append((max(n for link in (LOW, HIGH) for (_, c), n in at[link].items() if c in (2 * g, 2 * g + 1)), g))
    return [(min(n, last), g) for n, g in sorted(ends)]


def kernel(
    group_count,
    beta_list_hbm,
    beta_kind_hbm,
    opp_beta_kind_hbm,
    alpha_list_hbm,
    alpha_kind_hbm,
    opp_list_hbm,
    opp_kind_hbm,
    coeffs_hbm,
    beta_table_hbm,
    alpha_table_hbm,
    opp_alpha_table_hbm,
    opp_beta_table_hbm,
    out,
    beta_list,
    beta_kind,
    opp_beta_kind,
    alpha_list,
    alpha_kind,
    opp_list,
    opp_kind,
    coeffs,
    tables,
    plane,
    cross,
    sums,
    staged,
    passing,
    whole,
    half,
    acc,
    mine,
    tiles,
    onward,
    load_sem,
    plane_send,
    plane_recv,
    z_send,
    cross_recv,
    sum_send,
    pass_send,
    pass_recv,
    forward_send,
    hop_send,
    pair_send,
    pair_recv,
    half_send,
    half_recv,
):
    rows, cols = coeffs.shape
    kinds, tile = tables.shape[1:3]
    count = cols // tile
    relayed = count // 2
    summed = count - relayed
    plans = make_plans(summed, relayed)
    slots, _ = slots_of(plans)
    beta_table, alpha_table, opp_alpha_table, opp_beta_table = (tables.at[k] for k in range(4))
    me, core = lax.axis_index("alpha"), lax.axis_index("beta")
    z, p = me // GROUP, me % GROUP
    x, y = p % 2, p // 2
    places = (p + 1 - 2 * x, p + 2 - 4 * y, 3 - p)
    mates = tuple(z * GROUP + q for q in places)
    steps = (1 - 2 * x, 1 - 2 * y, 1 - 2 * y)
    middle = x + y == 1
    corner = jnp.logical_not(middle)

    def inside(group):
        return (group >= 0) & (group < group_count)

    has_out = [inside(z + step) for step in steps]
    has_in = [inside(z - step) for step in steps]

    def chip(index):
        return (index, core)

    pair = (me, 1 - core)

    def send(src, dst, send_sem, recv_sem, device):
        return pltpu.make_async_remote_copy(
            src_ref=src,
            dst_ref=dst,
            send_sem=send_sem,
            recv_sem=recv_sem,
            device_id=device,
            device_id_type=pl.DeviceIdType.MESH,
        )

    def sent(ref, sem):
        send(ref, ref, sem, sem, pair).wait_send()

    def arrived(ref, sem):
        send(ref, ref, sem, sem, pair).wait_recv()

    def columns(c):
        return pl.ds(c * tile, tile)

    def wide(g):
        return pl.ds(g * 2 * tile, 2 * tile)

    def both(g):
        return pl.ds(2 * g, 2)

    def own_copy(to, n, c):
        return send(
            coeffs.at[:, columns(c)],
            plane.at[to, c],
            plane_send,
            plane_recv.at[to, slots[to][n]],
            chip(mates[to]),
        )

    def relay_copy(to, n, c):
        return send(
            plane.at[HIGH if to == LOW else LOW, c],
            plane.at[DIAG, c],
            plane_send,
            plane_recv.at[to, slots[to][n]],
            chip(mates[to]),
        )

    def z_copy(r, c):
        return send(
            plane.at[r, c],
            cross.at[r, c],
            z_send.at[r],
            cross_recv.at[min(r, 1), c // 2],
            chip(me + GROUP * steps[r]),
        )

    def sum_copy(c):
        return send(staged.at[c], sums.at[c], sum_send, cross_recv.at[0, c // 2], chip(me + GROUP * steps[LOW]))

    def pass_copy(c):
        k = c - summed
        return send(
            coeffs.at[:, columns(c)], passing.at[k], pass_send, pass_recv, chip(me - GROUP * steps[HIGH])
        )

    def forward_copy(n, c):
        return send(
            passing.at[c - summed],
            cross.at[HIGH, c],
            forward_send,
            plane_recv.at[HIGH, slots[HIGH][n]],
            chip(mates[HIGH]),
        )

    def hop_copy(c):
        return send(cross.at[HIGH, c], cross.at[DIAG, c], hop_send, cross_recv.at[1, c // 2], chip(mates[LOW]))

    def half_copy(g):
        part = half.at[pl.ds(core * count + 2 * g, 2)]
        return send(part, part, half_send, half_recv, pair)

    def pair_copy(t):
        part = coeffs_hbm.at[:, pl.ds(t * tile, tile)]
        return send(part, whole.at[core * count + t], pair_send, pair_recv, pair)

    lists = (
        (alpha_list_hbm, alpha_list),
        (alpha_kind_hbm, alpha_kind),
        (opp_list_hbm, opp_list),
        (opp_kind_hbm, opp_kind),
        (beta_list_hbm, beta_list),
        (beta_kind_hbm, beta_kind),
        (opp_beta_kind_hbm, opp_beta_kind),
    )
    load_coeffs = pltpu.make_async_copy(coeffs_hbm, coeffs, load_sem.at[0])
    load_lists = [pltpu.make_async_copy(src, dst, load_sem.at[2 + k]) for k, (src, dst) in enumerate(lists)]
    load_coeffs.start()
    for load in load_lists:
        load.start()
    for k, src in enumerate((beta_table_hbm, alpha_table_hbm, opp_alpha_table_hbm, opp_beta_table_hbm)):
        pltpu.make_async_copy(src, tables.at[k], load_sem.at[1]).start()

    barrier = pltpu.get_barrier_semaphore()
    for device in (chip(mates[LOW]), chip(mates[HIGH]), pair):
        pl.semaphore_signal(barrier, inc=1, device_id=device, device_id_type=pl.DeviceIdType.MESH)
    up, down = inside(z + 1), inside(z - 1)
    for there, offset in ((up, GROUP), (down, -GROUP)):

        @pl.when(there)
        def _():
            pl.semaphore_signal(
                barrier, inc=1, device_id=chip(me + offset), device_id_type=pl.DeviceIdType.MESH
            )

    load_coeffs.wait()
    pl.semaphore_wait(barrier, 3 + up.astype(jnp.int32) + down.astype(jnp.int32))

    def issue(link, n):
        kind, c = plans[link][n]
        if kind == "o":
            own_copy(link, n, c).start()
        elif kind == "r":
            relay_copy(link, n, c).start()
        elif kind == "f":

            @pl.when(has_out[HIGH])
            def _():
                if c == summed:
                    arrived(passing, pass_recv)
                forward_copy(n, c).start()

        elif kind == "h":

            @pl.when(middle & has_in[HIGH])
            def _():
                hop_copy(c).start()

    times = issue_times(plans)

    def issue_after(i):
        due = [[(link, n) for n in range(last) for link in (LOW, HIGH) if when[link][n] == i] for when in times]
        if due[0] == due[1]:
            for link, n in due[0]:
                issue(link, n)
        else:
            for which in range(2):

                @pl.when(core == which)
                def _():
                    for link, n in due[which]:
                        issue(link, n)

    last = len(plans[LOW])
    issue_after(-1)

    @pl.when(has_in[HIGH])
    def _():
        for c in range(summed, count):
            pass_copy(c).start()

    for t in range(count):
        pair_copy(t).start()
    for load in load_lists:
        load.wait()
    pltpu.make_async_copy(tables, tables, load_sem.at[1]).wait()

    for t in range(count):
        whole[core * count + t] = coeffs[:, t * tile : (t + 1) * tile]

    for r in range(3):

        @pl.when(jnp.logical_not(has_in[r]))
        def _():
            cross[r] = jnp.zeros_like(cross[r])

    @pl.when(corner & jnp.logical_not(has_in[LOW]))
    def _():
        sums[...] = jnp.zeros_like(sums)

    sources = [me, mates[LOW], mates[DIAG], mates[HIGH]] + [mates[r] - GROUP * steps[r] for r in range(3)]
    for slot, source in enumerate(sources):
        at = pl.ds(slot * tile, tile)
        tiles[:tile, at] = picked_tile(me, alpha_list, alpha_kind, alpha_table, source).astype(BF16)
        tiles[tile:, at] = picked_tile(me, opp_list, opp_kind, opp_alpha_table, source).astype(BF16)

    summing = corner & has_out[LOW]

    @pl.when(summing)
    def _():
        target = me + GROUP * steps[LOW]
        for slot, source in enumerate(mates):
            at = pl.ds(slot * tile, tile)
            onward[:tile, at] = picked_tile(target, alpha_list, alpha_kind, alpha_table, source).astype(BF16)
            onward[tile:, at] = picked_tile(target, opp_list, opp_kind, opp_alpha_table, source).astype(BF16)

    def product(weights, first, blocks):
        return jnp.dot(
            weights[:, first * tile : (first + len(blocks)) * tile],
            jnp.concatenate(blocks, axis=0),
            preferred_element_type=F32,
        )

    def wide_block(ref, r, g):
        return jnp.concatenate([ref[r, 2 * g], ref[r, 2 * g + 1]], axis=1)

    def beta_apply(data, kind, table, j):
        left, right = [], []
        for link in range(beta_list.shape[0]):
            left.append(data[beta_list[link, j]])
            right.append(table[kind[link, j]])
        return lax.dot_general(
            jnp.concatenate(left, axis=1),
            jnp.concatenate(right, axis=1),
            (((1,), (1,)), ((), ())),
            preferred_element_type=F32,
        )

    def same_spin(j):
        mine[:, columns(j)] = beta_apply(whole, beta_kind, beta_table, j)

    def in_plane(g):
        blocks = [coeffs[:, wide(g)], wide_block(plane, LOW, g), wide_block(plane, DIAG, g)]
        if 2 * g < summed:
            blocks.append(wide_block(plane, HIGH, g))
        acc[:, wide(g)] = product(tiles, 0, blocks)

    def cross_wait(first, g, there=True):
        @pl.when(has_in[first] & there)
        def _():
            if first == LOW or 2 * g >= summed:
                arrived(cross.at[LOW if first == LOW else DIAG, both(g)], cross_recv.at[first, g])
            else:
                arrived(cross.at[pl.ds(HIGH, 2), both(g)], cross_recv.at[first, g])

    def settle(g, added):
        total = added
        for t in range(2):
            half[core * count + 2 * g + t] = total[tile:, t * tile : (t + 1) * tile].astype(BF16)
        mine[:, wide(g)] += total[:tile]

    def close(g):
        there = True if 2 * g >= summed else middle
        cross_wait(LOW, g, there)
        cross_wait(HIGH, g, there)
        if 2 * g < summed:

            @pl.when(corner & has_in[LOW])
            def _():
                arrived(sums.at[both(g)], cross_recv.at[0, g])

        if 2 * g >= summed:
            blocks = [wide_block(plane, HIGH, g), *(wide_block(cross, r, g) for r in range(3))]
            settle(g, acc[:, wide(g)] + product(tiles, 3, blocks))
        else:

            @pl.when(middle)
            def _():
                settle(g, acc[:, wide(g)] + product(tiles, 4, [wide_block(cross, r, g) for r in range(3)]))

            @pl.when(corner)
            def _():
                settle(g, acc[:, wide(g)] + jnp.concatenate([sums[2 * g], sums[2 * g + 1]], axis=1).astype(F32))

        half_copy(g).start()

    def sum_up(g):
        @pl.when(summing)
        def _():
            found = product(onward, 0, [wide_block(plane, r, g) for r in range(3)]).astype(BF16)
            for t in range(2):
                staged[2 * g + t] = found[:, t * tile : (t + 1) * tile]
                sum_copy(2 * g + t).start()

    seen = set()

    def take(link, n):
        kind, c = plans[link][n]
        if kind == "o":
            own_copy(link, n, c).wait_recv()
            if link == LOW:
                there = has_out[LOW] if c >= summed else has_out[LOW] & middle
            else:
                there = has_out[HIGH] & middle
            if link == LOW or c < summed:

                @pl.when(there)
                def _():
                    z_copy(link, c).start()

        elif kind == "r":
            relay_copy(link, n, c).wait_recv()

            @pl.when(middle & has_out[DIAG])
            def _():
                z_copy(DIAG, c).start()

            seen.add(c)
            if c ^ 1 in seen:
                if c < summed:
                    sum_up(c // 2)
                in_plane(c // 2)
        elif kind == "f":

            @pl.when(has_in[HIGH])
            def _():
                forward_copy(n, c).wait_recv()

    after = {i: [] for i in range(-1, last)}

    def put(i, what, *args):
        after[i].append((what, args))

    for j in range(count):
        put(-1, same_spin, j)
    for n, g in closing(plans, summed, relayed):
        put(n, close, g)

    arrived(whole.at[pl.ds((1 - core) * count, count)], pair_recv)
    for i in range(-1, last):
        if i >= 0:
            for link in (LOW, HIGH):
                take(link, i)
            issue_after(i)
        for what, args in after[i]:
            what(*args)

    arrived(half.at[pl.ds((1 - core) * count, count)], half_recv)
    for j in range(count):
        mixed = beta_apply(half, opp_beta_kind, opp_beta_table, j)
        out[:, columns(j)] = (mine[:, columns(j)] + mixed).astype(BF16)

    sent(plane, plane_send)
    sent(whole.at[pl.ds(0, count)], pair_send)
    sent(half.at[pl.ds(0, count)], half_send)

    @pl.when(has_in[HIGH])
    def _():
        sent(passing, pass_send)

    @pl.when(has_out[HIGH])
    def _():
        sent(passing, forward_send)

    @pl.when(middle & has_in[HIGH])
    def _():
        sent(passing, hop_send)

    @pl.when(middle & has_out[LOW])
    def _():
        sent(plane.at[LOW], z_send.at[LOW])

    @pl.when(middle & has_out[HIGH])
    def _():
        sent(plane.at[HIGH, pl.ds(0, summed)], z_send.at[HIGH])
        sent(plane.at[DIAG], z_send.at[DIAG])

    @pl.when(summing)
    def _():
        sent(plane.at[LOW, pl.ds(0, relayed)], z_send.at[LOW])
        sent(staged, sum_send)


def local(group_count, coeffs, *rest):
    lists, tables = rest[:7], rest[7:]
    flat = coeffs.reshape(coeffs.shape[1:])
    rows, cols = flat.shape
    kinds, tile = tables[0].shape[:2]
    count = cols // tile
    relayed, groups = count // 2, count // 2
    summed = count - relayed
    operands = tuple(
        pltpu.with_memory_space_constraint(one, pltpu.HBM) for one in (*(one.T for one in lists), flat, *tables)
    )
    in_lists = [pltpu.SMEM(one.shape, one.dtype) for one in operands[:7]]
    dma = pltpu.SemaphoreType.DMA
    result = pl.pallas_call(
        functools.partial(kernel, group_count),
        out_shape=jax.ShapeDtypeStruct((rows, cols), BF16),
        in_specs=[pl.BlockSpec(memory_space=pltpu.HBM)] * len(operands),
        out_specs=pl.BlockSpec(memory_space=pltpu.VMEM),
        scratch_shapes=[
            *in_lists,
            pltpu.VMEM((rows, cols), BF16),
            pltpu.VMEM((len(tables), *tables[0].shape), BF16),
            pltpu.VMEM((3, count, rows, tile), BF16),
            pltpu.VMEM((3, count, rows, tile), BF16),
            pltpu.VMEM((summed, 2 * rows, tile), BF16),
            pltpu.VMEM((summed, 2 * rows, tile), BF16),
            pltpu.VMEM((relayed, rows, tile), BF16),
            pltpu.VMEM((2 * count, rows, tile), BF16),
            pltpu.VMEM((2 * count, rows, tile), BF16),
            pltpu.VMEM((2 * tile, cols), F32),
            pltpu.VMEM((rows, cols), F32),
            pltpu.VMEM((2 * tile, 7 * tile), BF16),
            pltpu.VMEM((2 * tile, 3 * tile), BF16),
            dma((9,)),
            dma,
            dma((2, slots_of(make_plans(summed, relayed))[1])),
            dma((3,)),
            dma((2, groups)),
            dma,
            dma,
            dma,
            dma,
            dma,
            dma,
            dma,
            dma,
            dma,
        ],
        compiler_params=pltpu.CompilerParams(
            collective_id=0, has_side_effects=True, vmem_limit_bytes=20000 * 1024
        ),
    )(*operands)
    return result.reshape(coeffs.shape)


def solution(mesh):
    halves = P("beta", None)
    return jax.shard_map(
        functools.partial(local, mesh.shape["alpha"] // GROUP),
        mesh=mesh,
        in_specs=(P(None, "alpha", "beta"), halves, halves, halves) + (P(),) * 8,
        out_specs=P(None, "alpha", "beta"),
        check_vma=False,
    )
```

```python
import functools

import jax
import jax.numpy as jnp
from jax import lax
from jax.experimental import pallas as pl
from jax.experimental.pallas import tpu as pltpu
from jax.sharding import PartitionSpec as P

GROUP = 4
AHEAD = 6
FORWARD, STRIDE = 15, 7
DELAY = 4
SHIFT = 3
OPEN = (7, 5)
BF16, F32 = jnp.bfloat16, jnp.float32
LOW, HIGH, DIAG = range(3)


def picked_tile(block, lists, kinds, table, source):
    kind, found = jnp.int32(0), jnp.int32(0)
    for link in range(lists.shape[0]):
        hit = (lists[link, block] == source).astype(jnp.int32)
        kind += hit * kinds[link, block]
        found += hit
    return table[kind].astype(F32) * found.astype(F32)


def order_of(summed, relayed):
    spread = [(2 * g + 1, summed, "s", g) for g in range(summed // 2)]
    spread += [(2 * g + SHIFT, relayed, "r", g) for g in range(relayed // 2)]
    return [(kind, g) for _, _, kind, g in sorted(spread, key=lambda one: one[0] / one[1])]


def make_plans(summed, relayed):
    wanted = {LOW: [], HIGH: []}
    for kind, g in order_of(summed, relayed):
        first = 2 * g + (summed if kind == "r" else 0)
        wanted[LOW] += [first, first + 1]
        wanted[HIGH] += [first + 1, first]
    late = [c for c in wanted[HIGH] if c >= summed and c % 2 == 0]
    own = {LOW: list(wanted[LOW]), HIGH: [c for c in wanted[HIGH] if c not in late] + late}
    relays = {LOW: [c for c in wanted[HIGH] if c % 2 == 1], HIGH: [c for c in wanted[LOW] if c % 2 == 0]}
    plans, own_at, forward_at = ([], []), ({}, {}), []
    passed = hopped = n = 0
    while own[LOW] or own[HIGH] or relays[LOW] or relays[HIGH] or hopped < relayed:
        for link in (LOW, HIGH):
            other = HIGH if link == LOW else LOW
            due = passed < relayed and n >= FORWARD + STRIDE * passed // 4
            ready = relays[link] and own_at[other].get(relays[link][0], n) + AHEAD <= n
            spare = not own[link] or own[link][0] in late
            if ready:
                plans[link].append(("r", relays[link].pop(0)))
            elif link == HIGH and passed < relayed and (due or spare):
                plans[link].append(("f", summed + passed))
                forward_at.append(n)
                passed += 1
            elif own[link]:
                own_at[link][own[link][0]] = n
                plans[link].append(("o", own[link].pop(0)))
            elif link == LOW and hopped < passed and forward_at[hopped] + AHEAD <= n:
                plans[link].append(("h", summed + hopped))
                hopped += 1
            else:
                plans[link].append((None, None))
        n += 1
    return plans


def issue_times(plans):
    times = []
    for most in OPEN:
        per_link = ([], [])
        for link, plan in enumerate(plans):
            for n, (kind, c) in enumerate(plan):
                need = {"r": ("o", c), "h": ("f", c)}.get(kind)
                after = found_on(plans, 1 - link, need) if need else -1
                per_link[link].append(max([n - most, after, -1, *per_link[link][-1:]]))
        times.append(per_link)
    return times


def found_on(plans, link, item):
    return plans[link].index(item)


def slots_of(plans):
    times, slots, most = issue_times(plans), ([], []), 0
    for link, plan in enumerate(plans):
        held = []
        for n, (kind, _) in enumerate(plan):
            free = len(plan)
            for when in times:
                sure = [k for k in range(when[link][n] + 1) if plan[k][0] in ("o", "r")]
                free = min(free, when[link][sure[-1]] if sure else -1)
            if kind in ("o", "r", "f"):
                spot = next((k for k, user in enumerate(held) if user <= free), len(held))
                held[spot : spot + 1] = [n]
                slots[link].append(spot)
            else:
                slots[link].append(None)
        most = max(most, len(held))
    return slots, most


def closing(plans, summed, relayed):
    at = [{item: n for n, item in enumerate(plan)} for plan in plans]
    last = len(plans[LOW]) - 1
    free, ends = 0, []
    events = [(n, c) for (kind, c), n in at[LOW].items() if kind == "o" and c >= summed]
    for g in range(summed // 2):
        events.append((max(at[LOW]["r", 2 * g + 1], at[HIGH]["r", 2 * g]), 2 * g))
    for n, c in sorted(events):
        free = max(free, n) + (1 if c >= summed else 4)
        if c < summed:
            ends.append((free + DELAY, c // 2))
    for g in range(summed // 2, (summed + relayed) // 2):
        ends.append((max(n for link in (LOW, HIGH) for (_, c), n in at[link].items() if c in (2 * g, 2 * g + 1)), g))
    return [(min(n, last), g) for n, g in sorted(ends)]


def kernel(
    group_count,
    beta_list_hbm,
    beta_kind_hbm,
    opp_beta_kind_hbm,
    alpha_list_hbm,
    alpha_kind_hbm,
    opp_list_hbm,
    opp_kind_hbm,
    coeffs_hbm,
    beta_table_hbm,
    alpha_table_hbm,
    opp_alpha_table_hbm,
    opp_beta_table_hbm,
    out,
    beta_list,
    beta_kind,
    opp_beta_kind,
    alpha_list,
    alpha_kind,
    opp_list,
    opp_kind,
    coeffs,
    tables,
    plane,
    cross,
    sums,
    staged,
    passing,
    whole,
    half,
    acc,
    mine,
    tiles,
    onward,
    load_sem,
    own_send,
    plane_recv,
    relay_send,
    z_send,
    cross_recv,
    sum_send,
    pass_send,
    pass_recv,
    forward_send,
    hop_send,
    pair_send,
    pair_recv,
    half_send,
    half_recv,
):
    rows, cols = coeffs.shape
    kinds, tile = tables.shape[1:3]
    count = cols // tile
    relayed = count // 2
    summed = count - relayed
    plans = make_plans(summed, relayed)
    slots, _ = slots_of(plans)
    beta_table, alpha_table, opp_alpha_table, opp_beta_table = (tables.at[k] for k in range(4))
    me, core = lax.axis_index("alpha"), lax.axis_index("beta")
    z, p = me // GROUP, me % GROUP
    x, y = p % 2, p // 2
    places = (p + 1 - 2 * x, p + 2 - 4 * y, 3 - p)
    mates = tuple(z * GROUP + q for q in places)
    steps = (1 - 2 * x, 1 - 2 * y, 1 - 2 * y)
    middle = x + y == 1
    corner = jnp.logical_not(middle)

    def inside(group):
        return (group >= 0) & (group < group_count)

    has_out = [inside(z + step) for step in steps]
    has_in = [inside(z - step) for step in steps]

    def chip(index):
        return (index, core)

    pair = (me, 1 - core)

    def send(src, dst, send_sem, recv_sem, device):
        return pltpu.make_async_remote_copy(
            src_ref=src,
            dst_ref=dst,
            send_sem=send_sem,
            recv_sem=recv_sem,
            device_id=device,
            device_id_type=pl.DeviceIdType.MESH,
        )

    def sent(ref, sem):
        send(ref, ref, sem, sem, pair).wait_send()

    def arrived(ref, sem):
        send(ref, ref, sem, sem, pair).wait_recv()

    def columns(c):
        return pl.ds(c * tile, tile)

    def wide(g):
        return pl.ds(g * 2 * tile, 2 * tile)

    def both(g):
        return pl.ds(2 * g, 2)

    def own_copy(to, n, c):
        return send(
            coeffs.at[:, columns(c)],
            plane.at[to, c],
            own_send.at[to],
            plane_recv.at[to, slots[to][n]],
            chip(mates[to]),
        )

    def relay_copy(to, n, c):
        return send(
            plane.at[HIGH if to == LOW else LOW, c],
            plane.at[DIAG, c],
            relay_send,
            plane_recv.at[to, slots[to][n]],
            chip(mates[to]),
        )

    def z_copy(r, c):
        return send(
            plane.at[r, c],
            cross.at[r, c],
            z_send.at[r],
            cross_recv.at[min(r, 1), c // 2],
            chip(me + GROUP * steps[r]),
        )

    def sum_copy(c):
        return send(staged.at[c], sums.at[c], sum_send, cross_recv.at[0, c // 2], chip(me + GROUP * steps[LOW]))

    def pass_copy(c):
        k = c - summed
        return send(
            coeffs.at[:, columns(c)], passing.at[k], pass_send, pass_recv.at[k // 2], chip(me - GROUP * steps[HIGH])
        )

    def forward_copy(n, c):
        return send(
            passing.at[c - summed],
            cross.at[HIGH, c],
            forward_send,
            plane_recv.at[HIGH, slots[HIGH][n]],
            chip(mates[HIGH]),
        )

    def hop_copy(c):
        return send(cross.at[HIGH, c], cross.at[DIAG, c], hop_send, cross_recv.at[1, c // 2], chip(mates[LOW]))

    def half_copy(g):
        part = half.at[pl.ds(core * count + 2 * g, 2)]
        return send(part, part, half_send, half_recv, pair)

    def pair_copy(t):
        part = coeffs_hbm.at[:, pl.ds(t * tile, tile)]
        return send(part, whole.at[core * count + t], pair_send, pair_recv, pair)

    lists = (
        (alpha_list_hbm, alpha_list),
        (alpha_kind_hbm, alpha_kind),
        (opp_list_hbm, opp_list),
        (opp_kind_hbm, opp_kind),
        (beta_list_hbm, beta_list),
        (beta_kind_hbm, beta_kind),
        (opp_beta_kind_hbm, opp_beta_kind),
    )
    load_coeffs = pltpu.make_async_copy(coeffs_hbm, coeffs, load_sem.at[0])
    load_lists = [pltpu.make_async_copy(src, dst, load_sem.at[2 + k]) for k, (src, dst) in enumerate(lists)]
    load_coeffs.start()
    for load in load_lists:
        load.start()
    for k, src in enumerate((beta_table_hbm, alpha_table_hbm, opp_alpha_table_hbm, opp_beta_table_hbm)):
        pltpu.make_async_copy(src, tables.at[k], load_sem.at[1]).start()

    barrier = pltpu.get_barrier_semaphore()
    for device in (chip(mates[LOW]), chip(mates[HIGH]), pair):
        pl.semaphore_signal(barrier, inc=1, device_id=device, device_id_type=pl.DeviceIdType.MESH)
    up, down = inside(z + 1), inside(z - 1)
    for there, offset in ((up, GROUP), (down, -GROUP)):

        @pl.when(there)
        def _():
            pl.semaphore_signal(
                barrier, inc=1, device_id=chip(me + offset), device_id_type=pl.DeviceIdType.MESH
            )

    load_coeffs.wait()
    pl.semaphore_wait(barrier, 3 + up.astype(jnp.int32) + down.astype(jnp.int32))

    def issue(link, n):
        kind, c = plans[link][n]
        if kind == "o":
            own_copy(link, n, c).start()
        elif kind == "r":
            relay_copy(link, n, c).start()
        elif kind == "f":

            @pl.when(has_out[HIGH])
            def _():
                if c % 2 == 0:
                    k = c - summed
                    arrived(passing.at[pl.ds(k, 2)], pass_recv.at[k // 2])
                forward_copy(n, c).start()

        elif kind == "h":

            @pl.when(middle & has_in[HIGH])
            def _():
                hop_copy(c).start()

    times = issue_times(plans)

    def issue_after(i):
        due = [[(link, n) for n in range(last) for link in (LOW, HIGH) if when[link][n] == i] for when in times]
        if due[0] == due[1]:
            for link, n in due[0]:
                issue(link, n)
        else:
            for which in range(2):

                @pl.when(core == which)
                def _():
                    for link, n in due[which]:
                        issue(link, n)

    last = len(plans[LOW])
    issue_after(-1)

    @pl.when(has_in[HIGH])
    def _():
        for c in range(summed, count):
            pass_copy(c).start()

    for t in range(count):
        pair_copy(t).start()
    for load in load_lists:
        load.wait()
    pltpu.make_async_copy(tables, tables, load_sem.at[1]).wait()

    for t in range(count):
        whole[core * count + t] = coeffs[:, t * tile : (t + 1) * tile]

    for r in range(3):

        @pl.when(jnp.logical_not(has_in[r]))
        def _():
            cross[r] = jnp.zeros_like(cross[r])

    @pl.when(corner & jnp.logical_not(has_in[LOW]))
    def _():
        sums[...] = jnp.zeros_like(sums)

    sources = [me, mates[LOW], mates[DIAG], mates[HIGH]] + [mates[r] - GROUP * steps[r] for r in range(3)]
    for slot, source in enumerate(sources):
        at = pl.ds(slot * tile, tile)
        tiles[:tile, at] = picked_tile(me, alpha_list, alpha_kind, alpha_table, source).astype(BF16)
        tiles[tile:, at] = picked_tile(me, opp_list, opp_kind, opp_alpha_table, source).astype(BF16)

    summing = corner & has_out[LOW]

    @pl.when(summing)
    def _():
        target = me + GROUP * steps[LOW]
        for slot, source in enumerate(mates):
            at = pl.ds(slot * tile, tile)
            onward[:tile, at] = picked_tile(target, alpha_list, alpha_kind, alpha_table, source).astype(BF16)
            onward[tile:, at] = picked_tile(target, opp_list, opp_kind, opp_alpha_table, source).astype(BF16)

    def product(weights, first, blocks):
        return jnp.dot(
            weights[:, first * tile : (first + len(blocks)) * tile],
            jnp.concatenate(blocks, axis=0),
            preferred_element_type=F32,
        )

    def wide_block(ref, r, g):
        return jnp.concatenate([ref[r, 2 * g], ref[r, 2 * g + 1]], axis=1)

    def beta_apply(data, kind, table, j):
        left, right = [], []
        for link in range(beta_list.shape[0]):
            left.append(data[beta_list[link, j]])
            right.append(table[kind[link, j]])
        return lax.dot_general(
            jnp.concatenate(left, axis=1),
            jnp.concatenate(right, axis=1),
            (((1,), (1,)), ((), ())),
            preferred_element_type=F32,
        )

    def same_spin(j):
        mine[:, columns(j)] = beta_apply(whole, beta_kind, beta_table, j)

    def in_plane(g):
        blocks = [coeffs[:, wide(g)], wide_block(plane, LOW, g), wide_block(plane, DIAG, g)]
        if 2 * g < summed:
            blocks.append(wide_block(plane, HIGH, g))
        acc[:, wide(g)] = product(tiles, 0, blocks)

    def cross_wait(first, g, there=True):
        @pl.when(has_in[first] & there)
        def _():
            if first == LOW or 2 * g >= summed:
                arrived(cross.at[LOW if first == LOW else DIAG, both(g)], cross_recv.at[first, g])
            else:
                arrived(cross.at[pl.ds(HIGH, 2), both(g)], cross_recv.at[first, g])

    def settle(g, added):
        total = added
        for t in range(2):
            half[core * count + 2 * g + t] = total[tile:, t * tile : (t + 1) * tile].astype(BF16)
        mine[:, wide(g)] += total[:tile]

    def close(g):
        there = True if 2 * g >= summed else middle
        cross_wait(LOW, g, there)
        cross_wait(HIGH, g, there)
        if 2 * g < summed:

            @pl.when(corner & has_in[LOW])
            def _():
                arrived(sums.at[both(g)], cross_recv.at[0, g])

        if 2 * g >= summed:
            blocks = [wide_block(plane, HIGH, g), *(wide_block(cross, r, g) for r in range(3))]
            settle(g, acc[:, wide(g)] + product(tiles, 3, blocks))
        else:

            @pl.when(middle)
            def _():
                settle(g, acc[:, wide(g)] + product(tiles, 4, [wide_block(cross, r, g) for r in range(3)]))

            @pl.when(corner)
            def _():
                settle(g, acc[:, wide(g)] + jnp.concatenate([sums[2 * g], sums[2 * g + 1]], axis=1).astype(F32))

        half_copy(g).start()

    def sum_up(g):
        @pl.when(summing)
        def _():
            found = product(onward, 0, [wide_block(plane, r, g) for r in range(3)]).astype(BF16)
            for t in range(2):
                staged[2 * g + t] = found[:, t * tile : (t + 1) * tile]
                sum_copy(2 * g + t).start()

    seen = set()

    def take(link, n):
        kind, c = plans[link][n]
        if kind == "o":
            own_copy(link, n, c).wait_recv()
            if link == LOW:
                there = has_out[LOW] if c >= summed else has_out[LOW] & middle
            else:
                there = has_out[HIGH] & middle
            if link == LOW or c < summed:

                @pl.when(there)
                def _():
                    z_copy(link, c).start()

        elif kind == "r":
            relay_copy(link, n, c).wait_recv()

            @pl.when(middle & has_out[DIAG])
            def _():
                z_copy(DIAG, c).start()

            seen.add(c)
            if c ^ 1 in seen:
                if c < summed:
                    sum_up(c // 2)
                in_plane(c // 2)
        elif kind == "f":

            @pl.when(has_in[HIGH])
            def _():
                forward_copy(n, c).wait_recv()

    after = {i: [] for i in range(-1, last)}

    def put(i, what, *args):
        after[i].append((what, args))

    for j in range(count):
        put(-1, same_spin, j)
    for n, g in closing(plans, summed, relayed):
        put(n, close, g)

    arrived(whole.at[pl.ds((1 - core) * count, count)], pair_recv)
    for i in range(-1, last):
        if i >= 0:
            for link in (LOW, HIGH):
                take(link, i)
            issue_after(i)
        for what, args in after[i]:
            what(*args)

    arrived(half.at[pl.ds((1 - core) * count, count)], half_recv)
    for j in range(count):
        mixed = beta_apply(half, opp_beta_kind, opp_beta_table, j)
        out[:, columns(j)] = (mine[:, columns(j)] + mixed).astype(BF16)

    sent(coeffs, own_send.at[LOW])
    sent(coeffs, own_send.at[HIGH])
    sent(whole.at[pl.ds(0, count)], pair_send)
    sent(half.at[pl.ds(0, count)], half_send)
    sent(plane.at[DIAG], relay_send)

    @pl.when(has_in[HIGH])
    def _():
        sent(passing, pass_send)

    @pl.when(has_out[HIGH])
    def _():
        sent(passing, forward_send)

    @pl.when(middle & has_in[HIGH])
    def _():
        sent(passing, hop_send)

    @pl.when(middle & has_out[LOW])
    def _():
        sent(plane.at[LOW], z_send.at[LOW])

    @pl.when(middle & has_out[HIGH])
    def _():
        sent(plane.at[HIGH, pl.ds(0, summed)], z_send.at[HIGH])
        sent(plane.at[DIAG], z_send.at[DIAG])

    @pl.when(summing)
    def _():
        sent(plane.at[LOW, pl.ds(0, relayed)], z_send.at[LOW])
        sent(staged, sum_send)


def local(group_count, coeffs, *rest):
    lists, tables = rest[:7], rest[7:]
    flat = coeffs.reshape(coeffs.shape[1:])
    rows, cols = flat.shape
    kinds, tile = tables[0].shape[:2]
    count = cols // tile
    relayed, groups = count // 2, count // 2
    summed = count - relayed
    operands = tuple(
        pltpu.with_memory_space_constraint(one, pltpu.HBM) for one in (*(one.T for one in lists), flat, *tables)
    )
    in_lists = [pltpu.SMEM(one.shape, one.dtype) for one in operands[:7]]
    dma = pltpu.SemaphoreType.DMA
    result = pl.pallas_call(
        functools.partial(kernel, group_count),
        out_shape=jax.ShapeDtypeStruct((rows, cols), BF16),
        in_specs=[pl.BlockSpec(memory_space=pltpu.HBM)] * len(operands),
        out_specs=pl.BlockSpec(memory_space=pltpu.VMEM),
        scratch_shapes=[
            *in_lists,
            pltpu.VMEM((rows, cols), BF16),
            pltpu.VMEM((len(tables), *tables[0].shape), BF16),
            pltpu.VMEM((3, count, rows, tile), BF16),
            pltpu.VMEM((3, count, rows, tile), BF16),
            pltpu.VMEM((summed, 2 * rows, tile), BF16),
            pltpu.VMEM((summed, 2 * rows, tile), BF16),
            pltpu.VMEM((relayed, rows, tile), BF16),
            pltpu.VMEM((2 * count, rows, tile), BF16),
            pltpu.VMEM((2 * count, rows, tile), BF16),
            pltpu.VMEM((2 * tile, cols), F32),
            pltpu.VMEM((rows, cols), F32),
            pltpu.VMEM((2 * tile, 7 * tile), BF16),
            pltpu.VMEM((2 * tile, 3 * tile), BF16),
            dma((9,)),
            dma((2,)),
            dma((2, slots_of(make_plans(summed, relayed))[1])),
            dma,
            dma((3,)),
            dma((2, groups)),
            dma,
            dma,
            dma((relayed // 2,)),
            dma,
            dma,
            dma,
            dma,
            dma,
            dma,
        ],
        compiler_params=pltpu.CompilerParams(
            collective_id=0, has_side_effects=True, vmem_limit_bytes=20000 * 1024
        ),
    )(*operands)
    return result.reshape(coeffs.shape)


def solution(mesh):
    halves = P("beta", None)
    return jax.shard_map(
        functools.partial(local, mesh.shape["alpha"] // GROUP),
        mesh=mesh,
        in_specs=(P(None, "alpha", "beta"), halves, halves, halves) + (P(),) * 8,
        out_specs=P(None, "alpha", "beta"),
        check_vma=False,
    )
```
